512 devices in a mesh: gx: 16 (over y, core), gy: 8 (over z), gz: 4 (over x).
Axes of the slice: x: 4, y: 8, z: 8, core: 2. Of those that a mesh axis runs over, the one named last changes fastest.
Arguments:
- noise: float32 [32, 64, 64, 512], P(None, 'gx', 'gy', 'gz'), may hold values from -32 to 32
- basis: float32 [192, 64, 64, 512], P(None, 'gx', 'gy', 'gz'), may hold values from -5 to 5
- conductivity: float32 [64, 64, 512], P('gx', 'gy', 'gz'), may hold values from 0.2 to 2
- reaction: float32 [64, 64, 512], P('gx', 'gy', 'gz'), may hold values from 0.05 to 0.5
Outputs:
- new_block: float32 [32, 64, 64, 512], P(None, 'gx', 'gy', 'gz')
- factor: float32 [32, 32], replicated
- projection: float32 [192, 32], replicated
The draws below stay inside these ranges and needn't reach their ends.
All inputs are finite; a program needn't handle non-finite values.
Results may differ from the reference program's by a relative error of at most 0.00012.
Values sent between devices are 32-bit elements; how exact they have to be, the bound alone decides.
No kernel may reach another device: no remote copies, remote signals or barrier semaphores. Data moves between devices by JAX's collectives and lax.ppermute only.
A program may use at most 64 MiB of HBM per device.

```python
import math
import jax
import jax.numpy as jnp
from jax import lax

COLS = 32
BLOCKS = 6
BASIS = 192
NX = 64
NY = 64
NZ = 512


def basis_field(seed_key):
    shape = (BASIS, NX, NY, NZ)
    return jnp.clip(jax.random.normal(seed_key, shape), -5.0, 5.0)


def draw_basis(key, part):
    return basis_field(jax.random.fold_in(key, 11))


def draw_noise(key, part):
    stored = basis_field(jax.random.fold_in(key, 11)).reshape(BLOCKS, COLS, NX, NY, NZ)
    weights = jax.random.uniform(jax.random.fold_in(key, 12), (BLOCKS, COLS, 1, 1, 1), minval=0.3, maxval=0.7)
    fresh = jnp.clip(jax.random.normal(jax.random.fold_in(key, 13), (COLS, NX, NY, NZ)), -5.0, 5.0)
    return jnp.sum(weights * stored, axis=0) + 0.8 * fresh


def block_levels(key, shape, pieces, low, top_value):
    factor_of = 1.0
    for axis_at, shards_of in pieces:
        draws = jax.random.uniform(jax.random.fold_in(jax.random.fold_in(key, 6), axis_at), (shards_of,), jnp.float32, low / len(pieces), top_value / len(pieces))
        factor_of = factor_of * jnp.repeat(jnp.exp(draws), shape[axis_at] // shards_of).reshape((-1,) + (1,) * (len(shape) - 1 - axis_at))
    return factor_of


def setup_inputs(seed: int = 0) -> dict:
    splits = jax.random.split(jax.random.key(seed), 5)
    noise = draw_noise(jax.random.fold_in(splits[4], 71), 0)
    basis = draw_basis(jax.random.fold_in(splits[4], 71), 0)
    conductivity = jnp.clip(jnp.exp(math.log(2.0) - 2.3025851 * jax.random.uniform(splits[2], (NX, NY, NZ), jnp.float32) ** block_levels(splits[2], (NX, NY, NZ), ((0, 16), (1, 8), (2, 4)), -0.2, 0.2)), 0.2, 2.0)
    reaction = jnp.clip(jnp.exp(math.log(0.5) - 2.3025851 * jax.random.uniform(splits[3], (NX, NY, NZ), jnp.float32) ** block_levels(splits[3], (NX, NY, NZ), ((0, 16), (1, 8), (2, 4)), -0.2, 0.2)), 0.05, 0.5)
    return dict(noise=noise, basis=basis, conductivity=conductivity, reaction=reaction)


def stencil(field_pad, theta_pad, reaction_core):
    theta_core = theta_pad[1:-1, 1:-1, 1:-1]
    value_core = field_pad[:, 1:-1, 1:-1, 1:-1]
    result = reaction_core * value_core
    diagonal = reaction_core
    offsets = ((slice(2, None), slice(1, -1), slice(1, -1)), (slice(None, -2), slice(1, -1), slice(1, -1)), (slice(1, -1), slice(2, None), slice(1, -1)), (slice(1, -1), slice(None, -2), slice(1, -1)), (slice(1, -1), slice(1, -1), slice(2, None)), (slice(1, -1), slice(1, -1), slice(None, -2)))
    for slicer in offsets:
        face_value = 0.5 * (theta_core + theta_pad[slicer])
        result = result + face_value * (value_core - field_pad[(slice(None),) + slicer])
        diagonal = diagonal + face_value
    return (result, diagonal)

def reference(noise, basis, conductivity, reaction):
    highest = lax.Precision.HIGHEST
    cell_total = float(NX * NY * NZ)
    theta_pad = jnp.pad(conductivity, 1)
    widths = ((0, 0), (1, 1), (1, 1), (1, 1))
    first, diagonal = stencil(jnp.pad(noise, widths), theta_pad, reaction)
    scaled = first / diagonal
    image, unused = stencil(jnp.pad(scaled, widths), theta_pad, reaction)
    basis_flat = basis.reshape(BASIS, -1)
    image_flat = image.reshape(COLS, -1)

    def inner_product(left, right):
        return lax.dot_general(left, right, (((1,), (1,)), ((), ())), precision=highest) / cell_total

    def remove(block, coeff):
        return block - lax.dot_general(coeff, basis_flat, (((0,), (0,)), ((), ())), precision=highest)
    coeff_one = inner_product(basis_flat, image_flat)
    image_one = remove(image_flat, coeff_one)
    coeff_two = inner_product(basis_flat, image_one)
    image_two = remove(image_one, coeff_two)
    lower_one = jnp.linalg.cholesky(inner_product(image_two, image_two))
    middle = jax.scipy.linalg.solve_triangular(lower_one, image_two, lower=True)
    lower_two = jnp.linalg.cholesky(inner_product(middle, middle))
    new_block = jax.scipy.linalg.solve_triangular(lower_two, middle, lower=True)
    factor = jnp.dot(lower_two.T, lower_one.T, precision=highest)
    return (new_block.reshape(noise.shape), factor, coeff_one + coeff_two)
```

```python
import jax
import jax.numpy as jnp
from jax import lax
from jax.experimental import pallas as pl
from jax.experimental.pallas import tpu as pltpu
from jax.sharding import Mesh, PartitionSpec as P

GX = ("y", "core")
CHIP_X = ("core", "gz")
HIGHEST = lax.Precision.HIGHEST
F32 = jnp.float32


def shifted(value, axis, forward):
    size = lax.axis_size(axis)
    up = [(i, (i + 1) % size) for i in range(size - 1)]
    pairs = up if forward else [(j, i) for i, j in up]
    return lax.ppermute(value, axis, pairs)


def exchange(faces):
    xlo, xhi, ylo, yhi, zlo, zhi = faces
    return (
        shifted(xhi, GX, True),
        shifted(xlo, GX, False),
        shifted(yhi, "gy", True),
        shifted(ylo, "gy", False),
        shifted(zhi, "gz", True),
        shifted(zlo, "gz", False),
    )


def pack_faces(ref, row, rows, outs, at):
    xlo, xhi, ylo, yhi, zlo, zhi = outs
    fields, span_x, span_y, span_z = ref.shape
    xlo[at : at + fields] = ref[:, 0]
    xhi[at : at + fields] = ref[:, span_x - 1]
    ylo[at : at + fields] = ref[:, :, 0, :]
    yhi[at : at + fields] = ref[:, :, span_y - 1, :]
    step = min(rows, fields * span_x * span_y)
    per = step // (span_x * span_y)
    for k in range(fields // per):
        turned = ref[k * per : (k + 1) * per].reshape(step, span_z).T
        zlo[row + k : row + k + 1, :step] = turned[:1]
        zhi[row + k : row + k + 1, :step] = turned[span_z - 1 :]


def z_columns(low, high, row, step):
    lanes = low.shape[1]
    below = jnp.broadcast_to(low[row : row + 1, :step], (lanes, step))
    above = jnp.broadcast_to(high[row : row + 1, :step], (lanes, step))
    first = lax.broadcasted_iota(jnp.int32, (lanes, step), 0) < lanes // 2
    return jnp.where(first, below, above).T


def neighbours(value, halo, lo, hi, row, step):
    before_x, after_x, before_y, after_y, before_z, after_z = halo
    shape = value.shape
    span_y, span_z = shape[2:]
    at_y = lax.broadcasted_iota(jnp.int32, shape, 2)
    at_z = lax.broadcasted_iota(jnp.int32, shape, 3)
    x_minus = jnp.concatenate([before_x[lo:hi][:, None], value[:, :-1]], axis=1)
    x_plus = jnp.concatenate([value[:, 1:], after_x[lo:hi][:, None]], axis=1)
    y_minus = jnp.where(at_y == 0, before_y[lo:hi][:, :, None, :], pltpu.roll(value, 1, 2))
    y_plus = jnp.where(at_y == span_y - 1, after_y[lo:hi][:, :, None, :], pltpu.roll(value, span_y - 1, 2))
    edge = z_columns(before_z, after_z, row, step).reshape(shape)
    z_minus = jnp.where(at_z == 0, edge, pltpu.roll(value, 1, 3))
    z_plus = jnp.where(at_z == span_z - 1, edge, pltpu.roll(value, span_z - 1, 3))
    return (x_plus, x_minus, y_plus, y_minus, z_plus, z_minus)


def face_values(theta, halo, fields, rows):
    others = neighbours(theta[...][None], halo, fields, fields + 1, rows, theta.shape[0] * theta.shape[1])
    return [0.5 * (theta[...] + other[0]) for other in others]


def apply_operator(value, reaction, values, halo, lo, row, step):
    others = neighbours(value, halo, lo, lo + value.shape[0], row, step)
    result = reaction * value
    for face, other in zip(values, others):
        result = result + face * (value - other)
    return result


def face_kernel(noise, theta, *outs):
    fields = noise.shape[0]
    blocks = fields * noise.shape[1] * noise.shape[2] // 128
    pack_faces(noise, 0, 128, outs, 0)
    for ref, face in zip(outs[:2], (theta[0], theta[theta.shape[0] - 1])):
        ref[fields] = face
    outs[2][fields] = theta[:, 0, :]
    outs[3][fields] = theta[:, theta.shape[1] - 1, :]
    step = theta.shape[0] * theta.shape[1]
    turned = theta[...].reshape(step, theta.shape[2]).T
    outs[4][blocks : blocks + 1, :step] = turned[:1]
    outs[5][blocks : blocks + 1, :step] = turned[theta.shape[2] - 1 :]


def first_kernel(noise, theta, reaction, *refs):
    halo, scaled, outs = refs[:6], refs[6], refs[7:]
    fields, span_x, span_y, span_z = noise.shape
    blocks = fields * span_x * span_y // 128
    per = fields // blocks
    values = face_values(theta, halo, fields, blocks)
    diagonal = reaction[...]
    for face in values:
        diagonal = diagonal + face
    inverse = 1.0 / diagonal
    for k in range(blocks):
        value = noise[k * per : (k + 1) * per]
        first = apply_operator(value, reaction[...], values, halo, k * per, k, 128)
        scaled[k * per : (k + 1) * per] = first * inverse
    pack_faces(scaled, 0, 128, outs, 0)


def second_kernel(scaled, theta, reaction, *refs):
    halo, theta_halo, image = refs[:6], refs[6:12], refs[12]
    fields, span_x, span_y, span_z = scaled.shape
    blocks = fields * span_x * span_y // 128
    per = fields // blocks
    values = face_values(theta, theta_halo, fields, blocks)
    for k in range(blocks):
        value = scaled[k * per : (k + 1) * per]
        image[k * per : (k + 1) * per] = apply_operator(value, reaction[...], values, halo, k * per, k, 128)


def call(kernel, outs, *args):
    return pl.pallas_call(
        kernel,
        out_shape=[jax.ShapeDtypeStruct(s, F32) for s in outs],
        in_specs=[pl.BlockSpec(memory_space=pltpu.VMEM)] * len(args),
        out_specs=[pl.BlockSpec(memory_space=pltpu.VMEM)] * len(outs),
        cost_estimate=pl.CostEstimate(flops=1 << 22, bytes_accessed=1 << 21, transcendentals=0),
    )(*args)


def face_shapes(shape, extra):
    fields, span_x, span_y, span_z = shape
    n = fields + extra
    blocks = fields * span_x * span_y // 128
    z_rows = blocks + 8 * extra
    return [(n, span_y, span_z)] * 2 + [(n, span_x, span_z)] * 2 + [(z_rows, span_z)] * 2


def spread_sum(value, axes):
    size = lax.axis_size(axes)
    copies = jnp.broadcast_to(value[None], (size,) + value.shape)
    return jnp.sum(lax.all_to_all(copies, axes, 0, 0), axis=0)


def total(rows):
    size = lax.axis_size(CHIP_X)
    pieces = rows.reshape(size, -1, rows.shape[1])
    piece = jnp.sum(lax.all_to_all(pieces, CHIP_X, 0, 0), axis=0)
    piece = spread_sum(spread_sum(piece, "gy"), "y")
    copies = jnp.broadcast_to(piece[None], (size,) + piece.shape)
    return lax.all_to_all(copies, CHIP_X, 0, 0).reshape(rows.shape)


def shards(noise, basis, conductivity, reaction):
    columns = noise.shape[0]
    shape = noise.shape
    stored = basis.shape[0]
    cell_total = float(
        shape[1] * shape[2] * shape[3] * lax.axis_size(GX) * lax.axis_size("gy") * lax.axis_size("gz")
    )
    halo = exchange(call(face_kernel, face_shapes(shape, 1), noise, conductivity))
    scaled, *faces = call(
        first_kernel, [shape] + face_shapes(shape, 0), noise, conductivity, reaction, *halo
    )
    next_halo = exchange(faces)
    (image,) = call(second_kernel, [shape], scaled, conductivity, reaction, *next_halo, *halo)
    basis_flat = basis.reshape(stored, -1)
    image_flat = image.reshape(columns, -1)

    def dot(left, right, dims):
        return lax.dot_general(left, right, ((dims[0], dims[1]), ((), ())), precision=HIGHEST)

    rows_by_rows = ((1,), (1,))
    plain = ((1,), (0,))
    gram = dot(basis_flat, basis_flat, rows_by_rows)
    cross = dot(image_flat, basis_flat, rows_by_rows)
    own = dot(image_flat, image_flat, rows_by_rows)
    width = 128
    rest = stored - width
    corner = jnp.concatenate(
        [cross[:, width:], jnp.pad(own, ((0, rest - columns), (0, rest - columns)))], axis=0
    )[:rest]
    packed = jnp.concatenate(
        [
            gram[:, :width],
            cross[:, :width],
            jnp.concatenate([gram[width:, width:], corner], axis=1),
            jnp.zeros((32, width), F32),
        ],
        axis=0,
    )
    packed = total(packed) / cell_total
    left = packed[:stored]
    tail = packed[stored + columns : stored + columns + rest]
    gram = jnp.concatenate(
        [left, jnp.concatenate([left[width:].T, tail[:, :rest]], axis=0)], axis=1
    )
    one = jnp.concatenate([packed[stored : stored + columns], tail[:columns, rest:]], axis=1)
    own = tail[columns : 2 * columns, rest : rest + columns]
    two = one - dot(one, gram, plain)
    left_over = two - dot(two, gram, plain)
    both = one + two
    square = own - dot(one, both, rows_by_rows) - dot(both, left_over, rows_by_rows)
    eye = jnp.eye(columns, dtype=F32)
    lower_one = jnp.linalg.cholesky(square)
    inverse_one = jax.scipy.linalg.solve_triangular(lower_one, eye, lower=True)
    middle = dot(dot(inverse_one, square, plain), inverse_one, rows_by_rows)
    lower_two = jnp.linalg.cholesky(middle)
    inverse = jax.scipy.linalg.solve_triangular(lower_two, inverse_one, lower=True)
    factor = dot(lower_one, lower_two, plain).T
    mixed = dot(inverse, both, plain)
    new_block = dot(inverse, image_flat, plain) - dot(mixed, basis_flat, plain)
    return (new_block.reshape(shape), factor, both.T)


def solution(mesh):
    grid = mesh.devices.reshape(mesh.devices.shape[0] // 2, 2, *mesh.devices.shape[1:])
    fine = Mesh(grid, ("y", "core", "gy", "gz"))
    return jax.shard_map(
        shards,
        mesh=fine,
        in_specs=(
            P(None, GX, "gy", "gz"),
            P(None, GX, "gy", "gz"),
            P(GX, "gy", "gz"),
            P(GX, "gy", "gz"),
        ),
        out_specs=(P(None, GX, "gy", "gz"), P(), P()),
        check_vma=False,
    )
```

```python
import functools

import jax
import jax.numpy as jnp
from jax import lax
from jax.experimental import pallas as pl
from jax.experimental.pallas import tpu as pltpu
from jax.sharding import Mesh, PartitionSpec as P

GX = ("y", "core")
CHIP_X = ("core", "gz")
HIGHEST = lax.Precision.HIGHEST
F32 = jnp.float32
BF16 = jnp.bfloat16


def shifted(value, axis, forward):
    size = lax.axis_size(axis)
    up = [(i, (i + 1) % size) for i in range(size - 1)]
    pairs = up if forward else [(j, i) for i, j in up]
    return lax.ppermute(value, axis, pairs)


def exchange(faces):
    xlo, xhi, ylo, yhi, zlo, zhi = faces
    return (
        shifted(xhi, GX, True),
        shifted(xlo, GX, False),
        shifted(yhi, "gy", True),
        shifted(ylo, "gy", False),
        shifted(zhi, "gz", True),
        shifted(zlo, "gz", False),
    )


def pack_faces(ref, row, rows, outs, at):
    xlo, xhi, ylo, yhi, zlo, zhi = outs
    fields, span_x, span_y, span_z = ref.shape
    xlo[at : at + fields] = ref[:, 0]
    xhi[at : at + fields] = ref[:, span_x - 1]
    ylo[at : at + fields] = ref[:, :, 0, :]
    yhi[at : at + fields] = ref[:, :, span_y - 1, :]
    step = min(rows, fields * span_x * span_y)
    per = step // (span_x * span_y)
    for k in range(fields // per):
        turned = ref[k * per : (k + 1) * per].reshape(step, span_z).T
        zlo[row + k : row + k + 1, :step] = turned[:1]
        zhi[row + k : row + k + 1, :step] = turned[span_z - 1 :]


def z_columns(low, high, row, step):
    lanes = low.shape[1]
    below = jnp.broadcast_to(low[row : row + 1, :step], (lanes, step))
    above = jnp.broadcast_to(high[row : row + 1, :step], (lanes, step))
    first = lax.broadcasted_iota(jnp.int32, (lanes, step), 0) < lanes // 2
    return jnp.where(first, below, above).T


def neighbours(value, halo, lo, hi, row, step):
    before_x, after_x, before_y, after_y, before_z, after_z = halo
    shape = value.shape
    span_y, span_z = shape[2:]
    at_y = lax.broadcasted_iota(jnp.int32, shape, 2)
    at_z = lax.broadcasted_iota(jnp.int32, shape, 3)
    x_minus = jnp.concatenate([before_x[lo:hi][:, None], value[:, :-1]], axis=1)
    x_plus = jnp.concatenate([value[:, 1:], after_x[lo:hi][:, None]], axis=1)
    y_minus = jnp.where(at_y == 0, before_y[lo:hi][:, :, None, :], pltpu.roll(value, 1, 2))
    y_plus = jnp.where(at_y == span_y - 1, after_y[lo:hi][:, :, None, :], pltpu.roll(value, span_y - 1, 2))
    edge = z_columns(before_z, after_z, row, step).reshape(shape)
    z_minus = jnp.where(at_z == 0, edge, pltpu.roll(value, 1, 3))
    z_plus = jnp.where(at_z == span_z - 1, edge, pltpu.roll(value, span_z - 1, 3))
    return (x_plus, x_minus, y_plus, y_minus, z_plus, z_minus)


def face_values(theta, halo, fields, rows):
    others = neighbours(theta[...][None], halo, fields, fields + 1, rows, theta.shape[0] * theta.shape[1])
    return [0.5 * (theta[...] + other[0]) for other in others]


def apply_operator(value, reaction, values, halo, lo, row, step):
    others = neighbours(value, halo, lo, lo + value.shape[0], row, step)
    result = reaction * value
    for face, other in zip(values, others):
        result = result + face * (value - other)
    return result


def face_kernel(noise, theta, *outs):
    fields = noise.shape[0]
    blocks = fields * noise.shape[1] * noise.shape[2] // 128
    pack_faces(noise, 0, 128, outs, 0)
    for ref, face in zip(outs[:2], (theta[0], theta[theta.shape[0] - 1])):
        ref[fields] = face
    outs[2][fields] = theta[:, 0, :]
    outs[3][fields] = theta[:, theta.shape[1] - 1, :]
    step = theta.shape[0] * theta.shape[1]
    turned = theta[...].reshape(step, theta.shape[2]).T
    outs[4][blocks : blocks + 1, :step] = turned[:1]
    outs[5][blocks : blocks + 1, :step] = turned[theta.shape[2] - 1 :]


def first_kernel(noise, theta, reaction, *refs):
    halo, scaled, outs = refs[:6], refs[6], refs[7:]
    fields, span_x, span_y, span_z = noise.shape
    blocks = fields * span_x * span_y // 128
    per = fields // blocks
    values = face_values(theta, halo, fields, blocks)
    diagonal = reaction[...]
    for face in values:
        diagonal = diagonal + face
    inverse = 1.0 / diagonal
    for k in range(blocks):
        value = noise[k * per : (k + 1) * per]
        first = apply_operator(value, reaction[...], values, halo, k * per, k, 128)
        scaled[k * per : (k + 1) * per] = first * inverse
    pack_faces(scaled, 0, 128, outs, 0)


def split(value):
    high = value.astype(BF16)
    return high, (value - high.astype(F32)).astype(BF16)


def stacked(value):
    return jnp.concatenate(split(value), axis=0)


def contract(left, right, dims):
    return lax.dot_general(left, right, ((dims[0], dims[1]), ((), ())), preferred_element_type=F32)


def exact(left, right, dims):
    return lax.dot_general(
        left, right, ((dims[0], dims[1]), ((), ())), precision=HIGHEST, preferred_element_type=F32
    )


ROWS = ((1,), (1,))
PLAIN = ((1,), (0,))
COLUMNS = ((0,), (0,))


def basis_kernel(basis, high, low, packed):
    stored, span_x, span_y, span_z = basis.shape
    for a in range(span_x):
        for b in range(span_y):
            at = (a * span_y + b) * span_z
            high[:, at : at + span_z], low[:, at : at + span_z] = split(basis[:, a, b, :])
    top, rest = high[...], low[...]
    cross = contract(top, rest, ROWS)
    gram = contract(top, top, ROWS) + contract(rest, rest, ROWS) + (cross + cross.T)
    third = stored // 3
    packed[:third] = jnp.concatenate([gram[:third, :third], gram[2 * third :, 2 * third :]], axis=1)
    packed[third:] = gram[third:, : 2 * third]


def second_kernel(scaled, theta, reaction, *refs):
    halo, theta_halo = refs[:6], refs[6:12]
    gram, high, low, packed, own_high, own_low, image = refs[12:]
    fields, span_x, span_y, span_z = scaled.shape
    blocks = fields * span_x * span_y // 128
    per = fields // blocks
    values = face_values(theta, theta_halo, fields, blocks)
    for k in range(blocks):
        value = scaled[k * per : (k + 1) * per]
        image[k * per : (k + 1) * per] = apply_operator(value, reaction[...], values, halo, k * per, k, 128)
    stored = high.shape[0]
    for a in range(span_x):
        for b in range(span_y):
            at = (a * span_y + b) * span_z
            own_high[:, at : at + span_z], own_low[:, at : at + span_z] = split(image[:, a, b, :])
    both = jnp.concatenate([own_high[...], own_low[...]], axis=0)
    product = contract(high[...], both, ROWS) + contract(low[...], both, ROWS)
    product = product[:, :fields] + product[:, fields:]
    square = contract(both, both, ROWS)
    square = square[:fields] + square[fields:]
    square = square[:, :fields] + square[:, fields:]
    third = stored // 3
    own = jnp.concatenate([square, jnp.zeros((third - fields, fields), F32)], axis=0)
    packed[:stored] = gram[...]
    packed[stored:] = jnp.concatenate(
        [product[:third], product[third : 2 * third], product[2 * third : stored], own], axis=1
    )


def eliminate(square, right):
    size = square.shape[0]
    work = jnp.concatenate([0.5 * (square + square.T), right], axis=1)
    row = lax.broadcasted_iota(jnp.int32, work.shape, 0)
    lane = lax.broadcasted_iota(jnp.int32, work.shape, 1)
    for k in range(size - 1):
        column = jnp.broadcast_to(work[:, k : k + 1], work.shape)
        pivot = column[k : k + 1]
        work = work - jnp.where(row > k, column, 0.0) * (work[k : k + 1] / pivot)
    scale = jnp.sum(jnp.where(lane == row, work, 0.0), axis=1, keepdims=True)
    work = work / jnp.sqrt(scale)
    upper = jnp.where(lane >= row, work, 0.0)[:, :size]
    return upper, work[:, size:]


def finish_kernel(packed, high, low, own_high, own_low, new_block, factor, projection, *, cells):
    fields, span_x, span_y, span_z = new_block.shape
    stored = high.shape[0]
    third = stored // 3
    scaled = packed[...] * (1.0 / cells)
    top, body, tail = scaled[:third], scaled[third:stored], scaled[stored:]
    middle = body[:third, third:]
    first = jnp.concatenate([top[:, :third], body[:, :third].T], axis=1)
    second = jnp.concatenate([body[:third, :third], middle, body[third:, third:].T], axis=1)
    last = jnp.concatenate([body[third:], top[:, third:]], axis=1)
    gram = jnp.concatenate([first, second, last], axis=0)
    one = jnp.concatenate([tail[:, k * fields : (k + 1) * fields] for k in range(3)], axis=0)
    own = tail[:fields, 3 * fields :]
    two = one - exact(gram, one, PLAIN)
    left_over = two - exact(gram, two, PLAIN)
    both = one + two
    square = own - exact(one, both, COLUMNS) - exact(both, left_over, COLUMNS)
    row = lax.broadcasted_iota(jnp.int32, (fields, fields), 0)
    lane = lax.broadcasted_iota(jnp.int32, (fields, fields), 1)
    upper_one, inverse_one = eliminate(square, jnp.where(row == lane, 1.0, 0.0))
    again = exact(exact(inverse_one, 0.5 * (square + square.T), PLAIN), inverse_one, ROWS)
    upper_two, inverse = eliminate(again, inverse_one)
    factor[...] = exact(upper_two, upper_one, PLAIN)
    projection[...] = both.T
    mixed = stacked(exact(inverse, both, ROWS))
    inverse = stacked(inverse)
    width = span_y * span_z
    for a in range(span_x):
        at = a * width
        part = contract(inverse, own_high[:, at : at + width], PLAIN)
        part = part + contract(inverse, own_low[:, at : at + width], PLAIN)
        part = part - contract(mixed, high[:, at : at + width], PLAIN)
        part = part - contract(mixed, low[:, at : at + width], PLAIN)
        value = part[:fields] + part[fields:]
        for b in range(span_y):
            new_block[:, a, b, :] = value[:, b * span_z : (b + 1) * span_z]


def call(kernel, outs, *args, scratch=(), limit=16):
    return pl.pallas_call(
        kernel,
        out_shape=[o if isinstance(o, jax.ShapeDtypeStruct) else jax.ShapeDtypeStruct(o, F32) for o in outs],
        in_specs=[pl.BlockSpec(memory_space=pltpu.VMEM)] * len(args),
        out_specs=[pl.BlockSpec(memory_space=pltpu.VMEM)] * len(outs),
        scratch_shapes=list(scratch),
        compiler_params=pltpu.CompilerParams(vmem_limit_bytes=limit << 20),
        cost_estimate=pl.CostEstimate(flops=1 << 22, bytes_accessed=1 << 21, transcendentals=0),
    )(*args)


def face_shapes(shape, extra):
    fields, span_x, span_y, span_z = shape
    n = fields + extra
    blocks = fields * span_x * span_y // 128
    z_rows = blocks + 8 * extra
    return [(n, span_y, span_z)] * 2 + [(n, span_x, span_z)] * 2 + [(z_rows, span_z)] * 2


def spread_sum(value, axes):
    size = lax.axis_size(axes)
    copies = jnp.broadcast_to(value[None], (size,) + value.shape)
    return jnp.sum(lax.all_to_all(copies, axes, 0, 0), axis=0)


def total(rows):
    size = lax.axis_size(CHIP_X)
    pieces = rows.reshape(size, -1, rows.shape[1])
    piece = jnp.sum(lax.all_to_all(pieces, CHIP_X, 0, 0), axis=0)
    piece = spread_sum(spread_sum(piece, "gy"), "y")
    copies = jnp.broadcast_to(piece[None], (size,) + piece.shape)
    return lax.all_to_all(copies, CHIP_X, 0, 0).reshape(rows.shape)


def shards(noise, basis, conductivity, reaction):
    columns = noise.shape[0]
    shape = noise.shape
    stored = basis.shape[0]
    cell_total = float(
        shape[1] * shape[2] * shape[3] * lax.axis_size(GX) * lax.axis_size("gy") * lax.axis_size("gz")
    )
    halo = exchange(call(face_kernel, face_shapes(shape, 1), noise, conductivity))
    scaled, *faces = call(
        first_kernel, [shape] + face_shapes(shape, 0), noise, conductivity, reaction, *halo
    )
    next_halo = exchange(faces)
    cells = shape[1] * shape[2] * shape[3]
    third = stored // 3
    wide = jax.ShapeDtypeStruct((stored, cells), BF16)
    narrow = jax.ShapeDtypeStruct((columns, cells), BF16)
    high, low, gram = call(basis_kernel, [wide, wide, (stored, 2 * third)], basis)
    packed, own_high, own_low = call(
        second_kernel,
        [(stored + third, 2 * third), narrow, narrow],
        scaled,
        conductivity,
        reaction,
        *next_halo,
        *halo,
        gram,
        high,
        low,
        scratch=(pltpu.VMEM(shape, F32),),
    )
    new_block, factor, projection = call(
        functools.partial(finish_kernel, cells=cell_total),
        [shape, (columns, columns), (columns, stored)],
        total(packed),
        high,
        low,
        own_high,
        own_low,
    )
    return (new_block, factor, projection.T)


def solution(mesh):
    grid = mesh.devices.reshape(mesh.devices.shape[0] // 2, 2, *mesh.devices.shape[1:])
    fine = Mesh(grid, ("y", "core", "gy", "gz"))
    return jax.shard_map(
        shards,
        mesh=fine,
        in_specs=(
            P(None, GX, "gy", "gz"),
            P(None, GX, "gy", "gz"),
            P(GX, "gy", "gz"),
            P(GX, "gy", "gz"),
        ),
        out_specs=(P(None, GX, "gy", "gz"), P(), P()),
        check_vma=False,
    )
```

```python
import functools

import jax
import jax.numpy as jnp
from jax import lax
from jax.experimental import pallas as pl
from jax.experimental.pallas import tpu as pltpu
from jax.sharding import Mesh, PartitionSpec as P

GX = ("y", "core")
CHIP_X = ("core", "gz")
HIGHEST = lax.Precision.HIGHEST
F32 = jnp.float32
BF16 = jnp.bfloat16


def shifted(value, axis, forward):
    size = lax.axis_size(axis)
    up = [(i, (i + 1) % size) for i in range(size - 1)]
    pairs = up if forward else [(j, i) for i, j in up]
    return lax.ppermute(value, axis, pairs)


def exchange(faces):
    xlo, xhi, ylo, yhi, zlo, zhi = faces
    return (
        shifted(xhi, GX, True),
        shifted(xlo, GX, False),
        shifted(yhi, "gy", True),
        shifted(ylo, "gy", False),
        shifted(zhi, "gz", True),
        shifted(zlo, "gz", False),
    )


def across(ref, a, b):
    fields, span_x, span_y, span_z = ref.shape
    rows = ref.reshape(fields * span_x * span_y, span_z)
    return rows.at[pl.ds(a * span_y + b, fields, stride=span_x * span_y), :]


def pack_faces(ref, row, rows, outs, at):
    xlo, xhi, ylo, yhi, zlo, zhi = outs
    fields, span_x, span_y, span_z = ref.shape
    xlo[at : at + fields] = ref[:, 0]
    xhi[at : at + fields] = ref[:, span_x - 1]
    ylo[at : at + fields] = ref[:, :, 0, :]
    yhi[at : at + fields] = ref[:, :, span_y - 1, :]
    step = min(rows, fields * span_x * span_y)
    per = step // (span_x * span_y)
    for k in range(fields // per):
        turned = ref[k * per : (k + 1) * per].reshape(step, span_z).T
        zlo[row + k : row + k + 1, :step] = turned[:1]
        zhi[row + k : row + k + 1, :step] = turned[span_z - 1 :]


def z_columns(low, high, row, step):
    lanes = low.shape[1]
    below = jnp.broadcast_to(low[row : row + 1, :step], (lanes, step))
    above = jnp.broadcast_to(high[row : row + 1, :step], (lanes, step))
    first = lax.broadcasted_iota(jnp.int32, (lanes, step), 0) < lanes // 2
    return jnp.where(first, below, above).T


def neighbours(value, halo, lo, hi, row, step):
    before_x, after_x, before_y, after_y, before_z, after_z = halo
    shape = value.shape
    span_y, span_z = shape[2:]
    at_y = lax.broadcasted_iota(jnp.int32, shape, 2)
    at_z = lax.broadcasted_iota(jnp.int32, shape, 3)
    x_minus = jnp.concatenate([before_x[lo:hi][:, None], value[:, :-1]], axis=1)
    x_plus = jnp.concatenate([value[:, 1:], after_x[lo:hi][:, None]], axis=1)
    y_minus = jnp.where(at_y == 0, before_y[lo:hi][:, :, None, :], pltpu.roll(value, 1, 2))
    y_plus = jnp.where(at_y == span_y - 1, after_y[lo:hi][:, :, None, :], pltpu.roll(value, span_y - 1, 2))
    edge = z_columns(before_z, after_z, row, step).reshape(shape)
    z_minus = jnp.where(at_z == 0, edge, pltpu.roll(value, 1, 3))
    z_plus = jnp.where(at_z == span_z - 1, edge, pltpu.roll(value, span_z - 1, 3))
    return (x_plus, x_minus, y_plus, y_minus, z_plus, z_minus)


def face_values(theta, halo, fields, rows):
    others = neighbours(theta[...][None], halo, fields, fields + 1, rows, theta.shape[0] * theta.shape[1])
    return [0.5 * (theta[...] + other[0]) for other in others]


def apply_operator(value, reaction, values, halo, lo, row, step):
    others = neighbours(value, halo, lo, lo + value.shape[0], row, step)
    result = reaction * value
    for face, other in zip(values, others):
        result = result + face * (value - other)
    return result


def face_kernel(noise, theta, *outs):
    fields = noise.shape[0]
    blocks = fields * noise.shape[1] * noise.shape[2] // 128
    pack_faces(noise, 0, 128, outs, 0)
    for ref, face in zip(outs[:2], (theta[0], theta[theta.shape[0] - 1])):
        ref[fields] = face
    outs[2][fields] = theta[:, 0, :]
    outs[3][fields] = theta[:, theta.shape[1] - 1, :]
    step = theta.shape[0] * theta.shape[1]
    turned = theta[...].reshape(step, theta.shape[2]).T
    outs[4][blocks : blocks + 1, :step] = turned[:1]
    outs[5][blocks : blocks + 1, :step] = turned[theta.shape[2] - 1 :]


def first_kernel(noise, theta, reaction, *refs):
    halo, scaled, outs = refs[:6], refs[6], refs[7:]
    fields, span_x, span_y, span_z = noise.shape
    blocks = fields * span_x * span_y // 128
    per = fields // blocks
    values = face_values(theta, halo, fields, blocks)
    diagonal = reaction[...]
    for face in values:
        diagonal = diagonal + face
    inverse = 1.0 / diagonal
    for k in range(blocks):
        value = noise[k * per : (k + 1) * per]
        first = apply_operator(value, reaction[...], values, halo, k * per, k, 128)
        scaled[k * per : (k + 1) * per] = first * inverse
    pack_faces(scaled, 0, 128, outs, 0)


def split(value):
    high = value.astype(BF16)
    return high, (value - high.astype(F32)).astype(BF16)


def stacked(value):
    return jnp.concatenate(split(value), axis=0)


def contract(left, right, dims):
    return lax.dot_general(left, right, ((dims[0], dims[1]), ((), ())), preferred_element_type=F32)


def exact(left, right, dims):
    return lax.dot_general(
        left, right, ((dims[0], dims[1]), ((), ())), precision=HIGHEST, preferred_element_type=F32
    )


ROWS = ((1,), (1,))
PLAIN = ((1,), (0,))
COLUMNS = ((0,), (0,))


def basis_kernel(basis, high, low, packed):
    stored, span_x, span_y, span_z = basis.shape
    for a in range(span_x):
        for b in range(span_y):
            at = (a * span_y + b) * span_z
            high[:, at : at + span_z], low[:, at : at + span_z] = split(across(basis, a, b)[...])
    top, rest = high[...], low[...]
    cross = contract(top, rest, ROWS)
    gram = contract(top, top, ROWS) + contract(rest, rest, ROWS) + (cross + cross.T)
    third = stored // 3
    packed[:third] = jnp.concatenate([gram[:third, :third], gram[2 * third :, 2 * third :]], axis=1)
    packed[third:] = gram[third:, : 2 * third]


def second_kernel(scaled, theta, reaction, *refs):
    halo, theta_halo = refs[:6], refs[6:12]
    gram, high, low, packed, own_high, own_low, image = refs[12:]
    fields, span_x, span_y, span_z = scaled.shape
    blocks = fields * span_x * span_y // 128
    per = fields // blocks
    values = face_values(theta, theta_halo, fields, blocks)
    for k in range(blocks):
        value = scaled[k * per : (k + 1) * per]
        image[k * per : (k + 1) * per] = apply_operator(value, reaction[...], values, halo, k * per, k, 128)
    stored = high.shape[0]
    for a in range(span_x):
        for b in range(span_y):
            at = (a * span_y + b) * span_z
            own_high[:, at : at + span_z], own_low[:, at : at + span_z] = split(across(image, a, b)[...])
    both = jnp.concatenate([own_high[...], own_low[...]], axis=0)
    product = contract(high[...], both, ROWS) + contract(low[...], both, ROWS)
    product = product[:, :fields] + product[:, fields:]
    square = contract(both, both, ROWS)
    square = square[:fields] + square[fields:]
    square = square[:, :fields] + square[:, fields:]
    third = stored // 3
    own = jnp.concatenate([square, jnp.zeros((third - fields, fields), F32)], axis=0)
    packed[:stored] = gram[...]
    packed[stored:] = jnp.concatenate(
        [product[:third], product[third : 2 * third], product[2 * third : stored], own], axis=1
    )


def eliminate(square, right):
    size = square.shape[0]
    work = jnp.concatenate([0.5 * (square + square.T), right], axis=1)
    row = lax.broadcasted_iota(jnp.int32, work.shape, 0)
    lane = lax.broadcasted_iota(jnp.int32, work.shape, 1)
    for start in range(0, size, 8):
        columns = [jnp.broadcast_to(work[:, k : k + 1], work.shape) for k in range(start, start + 8)]
        for at in range(8):
            k = start + at
            inverse = 1.0 / columns[at][k : k + 1]
            below = jnp.where(row > k, columns[at], 0.0)
            work = work - below * (work[k : k + 1] * inverse)
            for later in range(at + 1, 8):
                columns[later] = columns[later] - below * (columns[later][k : k + 1] * inverse)
    scale = jnp.sum(jnp.where(lane == row, work, 0.0), axis=1, keepdims=True)
    work = work / jnp.sqrt(scale)
    upper = jnp.where(lane >= row, work, 0.0)[:, :size]
    return upper, work[:, size:]


def finish_kernel(packed, high, low, own_high, own_low, new_block, factor, projection, *, cells):
    fields, span_x, span_y, span_z = new_block.shape
    stored = high.shape[0]
    third = stored // 3
    scaled = packed[...] * (1.0 / cells)
    top, body, tail = scaled[:third], scaled[third:stored], scaled[stored:]
    middle = body[:third, third:]
    first = jnp.concatenate([top[:, :third], body[:, :third].T], axis=1)
    second = jnp.concatenate([body[:third, :third], middle, body[third:, third:].T], axis=1)
    last = jnp.concatenate([body[third:], top[:, third:]], axis=1)
    gram = jnp.concatenate([first, second, last], axis=0)
    one = jnp.concatenate([tail[:, k * fields : (k + 1) * fields] for k in range(3)], axis=0)
    own = tail[:fields, 3 * fields :]
    two = one - exact(gram, one, PLAIN)
    left_over = two - exact(gram, two, PLAIN)
    both = one + two
    square = own - exact(one, both, COLUMNS) - exact(both, left_over, COLUMNS)
    row = lax.broadcasted_iota(jnp.int32, (fields, fields), 0)
    lane = lax.broadcasted_iota(jnp.int32, (fields, fields), 1)
    upper_one, inverse_one = eliminate(square, jnp.where(row == lane, 1.0, 0.0))
    again = exact(exact(inverse_one, 0.5 * (square + square.T), PLAIN), inverse_one, ROWS)
    upper_two, inverse = eliminate(again, inverse_one)
    factor[...] = exact(upper_two, upper_one, PLAIN)
    projection[...] = both.T
    mixed = stacked(exact(inverse, both, ROWS))
    inverse = stacked(inverse)
    width = span_y * span_z
    for a in range(span_x):
        at = a * width
        part = contract(inverse, own_high[:, at : at + width], PLAIN)
        part = part + contract(inverse, own_low[:, at : at + width], PLAIN)
        part = part - contract(mixed, high[:, at : at + width], PLAIN)
        part = part - contract(mixed, low[:, at : at + width], PLAIN)
        value = part[:fields] + part[fields:]
        for b in range(span_y):
            across(new_block, a, b)[...] = value[:, b * span_z : (b + 1) * span_z]


def call(kernel, outs, *args, scratch=(), limit=16):
    return pl.pallas_call(
        kernel,
        out_shape=[o if isinstance(o, jax.ShapeDtypeStruct) else jax.ShapeDtypeStruct(o, F32) for o in outs],
        in_specs=[pl.BlockSpec(memory_space=pltpu.VMEM)] * len(args),
        out_specs=[pl.BlockSpec(memory_space=pltpu.VMEM)] * len(outs),
        scratch_shapes=list(scratch),
        compiler_params=pltpu.CompilerParams(vmem_limit_bytes=limit << 20),
        cost_estimate=pl.CostEstimate(flops=1 << 22, bytes_accessed=1 << 21, transcendentals=0),
    )(*args)


def face_shapes(shape, extra):
    fields, span_x, span_y, span_z = shape
    n = fields + extra
    blocks = fields * span_x * span_y // 128
    z_rows = blocks + 8 * extra
    return [(n, span_y, span_z)] * 2 + [(n, span_x, span_z)] * 2 + [(z_rows, span_z)] * 2


def spread_sum(value, axes):
    size = lax.axis_size(axes)
    copies = jnp.broadcast_to(value[None], (size,) + value.shape)
    return jnp.sum(lax.all_to_all(copies, axes, 0, 0), axis=0)


def total(rows):
    size = lax.axis_size(CHIP_X)
    pieces = rows.reshape(size, -1, rows.shape[1])
    piece = jnp.sum(lax.all_to_all(pieces, CHIP_X, 0, 0), axis=0)
    piece = spread_sum(spread_sum(piece, "gy"), "y")
    copies = jnp.broadcast_to(piece[None], (size,) + piece.shape)
    return lax.all_to_all(copies, CHIP_X, 0, 0).reshape(rows.shape)


def shards(noise, basis, conductivity, reaction):
    columns = noise.shape[0]
    shape = noise.shape
    stored = basis.shape[0]
    cell_total = float(
        shape[1] * shape[2] * shape[3] * lax.axis_size(GX) * lax.axis_size("gy") * lax.axis_size("gz")
    )
    halo = exchange(call(face_kernel, face_shapes(shape, 1), noise, conductivity))
    scaled, *faces = call(
        first_kernel, [shape] + face_shapes(shape, 0), noise, conductivity, reaction, *halo
    )
    next_halo = exchange(faces)
    cells = shape[1] * shape[2] * shape[3]
    third = stored // 3
    wide = jax.ShapeDtypeStruct((stored, cells), BF16)
    narrow = jax.ShapeDtypeStruct((columns, cells), BF16)
    high, low, gram = call(basis_kernel, [wide, wide, (stored, 2 * third)], basis)
    packed, own_high, own_low = call(
        second_kernel,
        [(stored + third, 2 * third), narrow, narrow],
        scaled,
        conductivity,
        reaction,
        *next_halo,
        *halo,
        gram,
        high,
        low,
        scratch=(pltpu.VMEM(shape, F32),),
    )
    new_block, factor, projection = call(
        functools.partial(finish_kernel, cells=cell_total),
        [shape, (columns, columns), (columns, stored)],
        total(packed),
        high,
        low,
        own_high,
        own_low,
    )
    return (new_block, factor, projection.T)


def solution(mesh):
    grid = mesh.devices.reshape(mesh.devices.shape[0] // 2, 2, *mesh.devices.shape[1:])
    fine = Mesh(grid, ("y", "core", "gy", "gz"))
    return jax.shard_map(
        shards,
        mesh=fine,
        in_specs=(
            P(None, GX, "gy", "gz"),
            P(None, GX, "gy", "gz"),
            P(GX, "gy", "gz"),
            P(GX, "gy", "gz"),
        ),
        out_specs=(P(None, GX, "gy", "gz"), P(), P()),
        check_vma=False,
    )
```

```python
import functools

import jax
import jax.numpy as jnp
from jax import lax
from jax.experimental import pallas as pl
from jax.experimental.pallas import tpu as pltpu
from jax.sharding import Mesh, PartitionSpec as P

GX = ("y", "core")
SCATTER = ("core", "gy")
REST = ("y", "gz")
HIGHEST = lax.Precision.HIGHEST
F32 = jnp.float32
BF16 = jnp.bfloat16


def shifted(value, axis, forward):
    size = lax.axis_size(axis)
    up = [(i, (i + 1) % size) for i in range(size - 1)]
    pairs = up if forward else [(j, i) for i, j in up]
    return lax.ppermute(value, axis, pairs)


def exchange(faces):
    xlo, xhi, ylo, yhi, zlo, zhi = faces
    return (
        shifted(xhi, GX, True),
        shifted(xlo, GX, False),
        shifted(yhi, "gy", True),
        shifted(ylo, "gy", False),
        shifted(zhi, "gz", True),
        shifted(zlo, "gz", False),
    )


def across(ref, a, b):
    fields, span_x, span_y, span_z = ref.shape
    rows = ref.reshape(fields * span_x * span_y, span_z)
    return rows.at[pl.ds(a * span_y + b, fields, stride=span_x * span_y), :]


def pack_faces(ref, row, rows, outs, at):
    xlo, xhi, ylo, yhi, zlo, zhi = outs
    fields, span_x, span_y, span_z = ref.shape
    xlo[at : at + fields] = ref[:, 0]
    xhi[at : at + fields] = ref[:, span_x - 1]
    ylo[at : at + fields] = ref[:, :, 0, :]
    yhi[at : at + fields] = ref[:, :, span_y - 1, :]
    step = min(rows, fields * span_x * span_y)
    per = step // (span_x * span_y)
    for k in range(fields // per):
        turned = ref[k * per : (k + 1) * per].reshape(step, span_z).T
        zlo[row + k : row + k + 1, :step] = turned[:1]
        zhi[row + k : row + k + 1, :step] = turned[span_z - 1 :]


def z_columns(low, high, row, step):
    lanes = low.shape[1]
    below = jnp.broadcast_to(low[row : row + 1, :step], (lanes, step))
    above = jnp.broadcast_to(high[row : row + 1, :step], (lanes, step))
    first = lax.broadcasted_iota(jnp.int32, (lanes, step), 0) < lanes // 2
    return jnp.where(first, below, above).T


def neighbours(value, halo, lo, hi, row, step):
    before_x, after_x, before_y, after_y, before_z, after_z = halo
    shape = value.shape
    span_y, span_z = shape[2:]
    at_y = lax.broadcasted_iota(jnp.int32, shape, 2)
    at_z = lax.broadcasted_iota(jnp.int32, shape, 3)
    x_minus = jnp.concatenate([before_x[lo:hi][:, None], value[:, :-1]], axis=1)
    x_plus = jnp.concatenate([value[:, 1:], after_x[lo:hi][:, None]], axis=1)
    y_minus = jnp.where(at_y == 0, before_y[lo:hi][:, :, None, :], pltpu.roll(value, 1, 2))
    y_plus = jnp.where(at_y == span_y - 1, after_y[lo:hi][:, :, None, :], pltpu.roll(value, span_y - 1, 2))
    edge = z_columns(before_z, after_z, row, step).reshape(shape)
    z_minus = jnp.where(at_z == 0, edge, pltpu.roll(value, 1, 3))
    z_plus = jnp.where(at_z == span_z - 1, edge, pltpu.roll(value, span_z - 1, 3))
    return (x_plus, x_minus, y_plus, y_minus, z_plus, z_minus)


def face_values(theta, halo, fields, rows):
    others = neighbours(theta[...][None], halo, fields, fields + 1, rows, theta.shape[0] * theta.shape[1])
    return [0.5 * (theta[...] + other[0]) for other in others]


def apply_operator(value, reaction, values, halo, lo, row, step):
    others = neighbours(value, halo, lo, lo + value.shape[0], row, step)
    result = reaction * value
    for face, other in zip(values, others):
        result = result + face * (value - other)
    return result


def face_kernel(noise_hbm, theta_hbm, reaction_hbm, noise, theta, reaction, *refs):
    outs, sem = refs[:6], refs[6]
    loads = [
        pltpu.make_async_copy(source, target, sem.at[k])
        for k, (source, target) in enumerate(
            ((noise_hbm, noise), (theta_hbm, theta), (reaction_hbm, reaction))
        )
    ]
    for load in loads:
        load.start()
    for load in loads:
        load.wait()
    fields = noise.shape[0]
    blocks = fields * noise.shape[1] * noise.shape[2] // 128
    pack_faces(noise, 0, 128, outs, 0)
    for ref, face in zip(outs[:2], (theta[0], theta[theta.shape[0] - 1])):
        ref[fields] = face
    outs[2][fields] = theta[:, 0, :]
    outs[3][fields] = theta[:, theta.shape[1] - 1, :]
    step = theta.shape[0] * theta.shape[1]
    turned = theta[...].reshape(step, theta.shape[2]).T
    outs[4][blocks : blocks + 1, :step] = turned[:1]
    outs[5][blocks : blocks + 1, :step] = turned[theta.shape[2] - 1 :]


def first_kernel(noise, theta, reaction, *refs):
    halo, scaled, outs = refs[:6], refs[6], refs[7:]
    fields, span_x, span_y, span_z = noise.shape
    blocks = fields * span_x * span_y // 128
    per = fields // blocks
    values = face_values(theta, halo, fields, blocks)
    diagonal = reaction[...]
    for face in values:
        diagonal = diagonal + face
    inverse = 1.0 / diagonal
    for k in range(blocks):
        value = noise[k * per : (k + 1) * per]
        first = apply_operator(value, reaction[...], values, halo, k * per, k, 128)
        scaled[k * per : (k + 1) * per] = first * inverse
    pack_faces(scaled, 0, 128, outs, 0)


def split(value):
    high = value.astype(BF16)
    return high, (value - high.astype(F32)).astype(BF16)


def stacked(value):
    return jnp.concatenate(split(value), axis=0)


def contract(left, right, dims):
    return lax.dot_general(left, right, ((dims[0], dims[1]), ((), ())), preferred_element_type=F32)


def exact(left, right, dims):
    return lax.dot_general(
        left, right, ((dims[0], dims[1]), ((), ())), precision=HIGHEST, preferred_element_type=F32
    )


ROWS = ((1,), (1,))
PLAIN = ((1,), (0,))
COLUMNS = ((0,), (0,))


def basis_kernel(basis_hbm, high, low, packed, basis, sem):
    stored, span_x, span_y, span_z = basis.shape
    chunk = stored // sem.shape[0]
    loads = [
        pltpu.make_async_copy(basis_hbm.at[pl.ds(k * chunk, chunk)], basis.at[pl.ds(k * chunk, chunk)], sem.at[k])
        for k in range(sem.shape[0])
    ]
    for load in loads:
        load.start()
    for k, load in enumerate(loads):
        load.wait()
        part = basis.at[pl.ds(k * chunk, chunk)]
        rows = slice(k * chunk, (k + 1) * chunk)
        for a in range(span_x):
            for b in range(span_y):
                at = (a * span_y + b) * span_z
                high[rows, at : at + span_z], low[rows, at : at + span_z] = split(across(part, a, b)[...])
    top, rest = high[...], low[...]
    cross = contract(top, rest, ROWS)
    gram = contract(top, top, ROWS) + contract(rest, rest, ROWS) + (cross + cross.T)
    third = stored // 3
    packed[:third] = jnp.concatenate([gram[:third, :third], gram[2 * third :, 2 * third :]], axis=1)
    packed[third:] = gram[third:, : 2 * third]


def second_kernel(scaled, theta, reaction, *refs):
    halo, theta_halo, own, image = refs[:6], refs[6:12], refs[12], refs[13]
    fields, span_x, span_y, span_z = scaled.shape
    blocks = fields * span_x * span_y // 128
    per = fields // blocks
    values = face_values(theta, theta_halo, fields, blocks)
    for k in range(blocks):
        value = scaled[k * per : (k + 1) * per]
        image[k * per : (k + 1) * per] = apply_operator(value, reaction[...], values, halo, k * per, k, 128)
    for a in range(span_x):
        for b in range(span_y):
            at = (a * span_y + b) * span_z
            own[:fields, at : at + span_z], own[fields:, at : at + span_z] = split(across(image, a, b)[...])


def product_kernel(gram, high, low, own, packed):
    stored, fields = high.shape[0], own.shape[0] // 2
    both = own[...]
    product = contract(high[...], both, ROWS) + contract(low[...], both, ROWS)
    product = product[:, :fields] + product[:, fields:]
    square = contract(both, both, ROWS)
    square = square[:fields] + square[fields:]
    square = square[:, :fields] + square[:, fields:]
    third = stored // 3
    last = jnp.concatenate([square, jnp.zeros((third - fields, fields), F32)], axis=0)
    packed[:stored] = gram[...]
    packed[stored:] = jnp.concatenate(
        [product[:third], product[third : 2 * third], product[2 * third : stored], last], axis=1
    )


def eliminate(square, right):
    size = square.shape[0]
    work = jnp.concatenate([0.5 * (square + square.T), right], axis=1)
    row = lax.broadcasted_iota(jnp.int32, work.shape, 0)
    lane = lax.broadcasted_iota(jnp.int32, work.shape, 1)
    for start in range(0, size, 8):
        columns = [jnp.broadcast_to(work[:, k : k + 1], work.shape) for k in range(start, start + 8)]
        for at in range(8):
            k = start + at
            inverse = 1.0 / columns[at][k : k + 1]
            below = jnp.where(row > k, columns[at], 0.0)
            work = work - below * (work[k : k + 1] * inverse)
            for later in range(at + 1, 8):
                columns[later] = columns[later] - below * (columns[later][k : k + 1] * inverse)
    scale = jnp.sum(jnp.where(lane == row, work, 0.0), axis=1, keepdims=True)
    work = work / jnp.sqrt(scale)
    upper = jnp.where(lane >= row, work, 0.0)[:, :size]
    return upper, work[:, size:]


def finish_kernel(packed, high, low, image_hbm, new_block, factor, projection, image, sem, *, cells):
    load = pltpu.make_async_copy(image_hbm, image, sem)
    load.start()
    fields, span_x, span_y, span_z = new_block.shape
    stored = high.shape[0]
    third = stored // 3
    scaled = packed[...] * (1.0 / cells)
    top, body, tail = scaled[:third], scaled[third:stored], scaled[stored:]
    middle = body[:third, third:]
    first = jnp.concatenate([top[:, :third], body[:, :third].T], axis=1)
    second = jnp.concatenate([body[:third, :third], middle, body[third:, third:].T], axis=1)
    last = jnp.concatenate([body[third:], top[:, third:]], axis=1)
    gram = jnp.concatenate([first, second, last], axis=0)
    one = jnp.concatenate([tail[:, k * fields : (k + 1) * fields] for k in range(3)], axis=0)
    own = tail[:fields, 3 * fields :]
    two = one - exact(gram, one, PLAIN)
    left_over = two - exact(gram, two, PLAIN)
    both = one + two
    square = own - exact(one, both, COLUMNS) - exact(both, left_over, COLUMNS)
    row = lax.broadcasted_iota(jnp.int32, (fields, fields), 0)
    lane = lax.broadcasted_iota(jnp.int32, (fields, fields), 1)
    upper_one, inverse_one = eliminate(square, jnp.where(row == lane, 1.0, 0.0))
    again = exact(exact(inverse_one, 0.5 * (square + square.T), PLAIN), inverse_one, ROWS)
    upper_two, inverse = eliminate(again, inverse_one)
    factor[...] = exact(upper_two, upper_one, PLAIN)
    projection[...] = both.T
    mixed = stacked(exact(inverse, both, ROWS))
    inverse = stacked(inverse)
    width = span_y * span_z
    load.wait()
    for a in range(span_x):
        at = a * width
        part = contract(inverse, image[:fields, at : at + width], PLAIN)
        part = part + contract(inverse, image[fields:, at : at + width], PLAIN)
        part = part - contract(mixed, high[:, at : at + width], PLAIN)
        part = part - contract(mixed, low[:, at : at + width], PLAIN)
        value = part[:fields] + part[fields:]
        for b in range(span_y):
            across(new_block, a, b)[...] = value[:, b * span_z : (b + 1) * span_z]


def call(kernel, outs, *args, scratch=(), hbm=(), limit=16, cost=1 << 21):
    return pl.pallas_call(
        kernel,
        out_shape=[o if isinstance(o, jax.ShapeDtypeStruct) else jax.ShapeDtypeStruct(o, F32) for o in outs],
        in_specs=[pl.BlockSpec(memory_space=pltpu.HBM if k in hbm else pltpu.VMEM) for k in range(len(args))],
        out_specs=[pl.BlockSpec(memory_space=pltpu.VMEM)] * len(outs),
        scratch_shapes=list(scratch),
        compiler_params=pltpu.CompilerParams(vmem_limit_bytes=limit << 20),
        cost_estimate=pl.CostEstimate(flops=1 << 22, bytes_accessed=cost, transcendentals=0),
    )(*(pltpu.with_memory_space_constraint(a, pltpu.HBM) if k in hbm else a for k, a in enumerate(args)))


def face_shapes(shape, extra):
    fields, span_x, span_y, span_z = shape
    n = fields + extra
    blocks = fields * span_x * span_y // 128
    z_rows = blocks + 8 * extra
    return [(n, span_y, span_z)] * 2 + [(n, span_x, span_z)] * 2 + [(z_rows, span_z)] * 2


def spread_sum(value, axes):
    size = lax.axis_size(axes)
    copies = jnp.broadcast_to(value[None], (size,) + value.shape)
    return jnp.sum(lax.all_to_all(copies, axes, 0, 0), axis=0)


def total(rows):
    size = lax.axis_size(SCATTER)
    pieces = rows.reshape(size, -1, rows.shape[1])
    piece = jnp.sum(lax.all_to_all(pieces, SCATTER, 0, 0), axis=0)
    piece = spread_sum(piece, REST)
    copies = jnp.broadcast_to(piece[None], (size,) + piece.shape)
    return lax.all_to_all(copies, SCATTER, 0, 0).reshape(rows.shape)


def shards(noise, basis, conductivity, reaction):
    columns = noise.shape[0]
    shape = noise.shape
    stored = basis.shape[0]
    cell_total = float(
        shape[1] * shape[2] * shape[3] * lax.axis_size(GX) * lax.axis_size("gy") * lax.axis_size("gz")
    )
    noise, conductivity, reaction, *faces = call(
        face_kernel,
        [shape, conductivity.shape, reaction.shape] + face_shapes(shape, 1),
        noise,
        conductivity,
        reaction,
        scratch=(pltpu.SemaphoreType.DMA((3,)),),
        hbm=(0, 1, 2),
    )
    halo = exchange(faces)
    scaled, *faces = call(
        first_kernel, [shape] + face_shapes(shape, 0), noise, conductivity, reaction, *halo, cost=1 << 24
    )
    next_halo = exchange(faces)
    cells = shape[1] * shape[2] * shape[3]
    third = stored // 3
    wide = jax.ShapeDtypeStruct((stored, cells), BF16)
    high, low, gram = call(
        basis_kernel,
        [wide, wide, (stored, 2 * third)],
        basis,
        scratch=(pltpu.VMEM(basis.shape, F32), pltpu.SemaphoreType.DMA((6,))),
        hbm=(0,),
    )
    (own,) = call(
        second_kernel,
        [jax.ShapeDtypeStruct((2 * columns, cells), BF16)],
        scaled,
        conductivity,
        reaction,
        *next_halo,
        *halo,
        scratch=(pltpu.VMEM(shape, F32),),
    )
    (packed,) = call(product_kernel, [(stored + third, 2 * third)], gram, high, low, own)
    new_block, factor, projection = call(
        functools.partial(finish_kernel, cells=cell_total),
        [shape, (columns, columns), (columns, stored)],
        total(packed),
        high,
        low,
        own,
        scratch=(pltpu.VMEM(own.shape, BF16), pltpu.SemaphoreType.DMA),
        hbm=(3,),
    )
    return (new_block, factor, projection.T)


def solution(mesh):
    grid = mesh.devices.reshape(mesh.devices.shape[0] // 2, 2, *mesh.devices.shape[1:])
    fine = Mesh(grid, ("y", "core", "gy", "gz"))
    return jax.shard_map(
        shards,
        mesh=fine,
        in_specs=(
            P(None, GX, "gy", "gz"),
            P(None, GX, "gy", "gz"),
            P(GX, "gy", "gz"),
            P(GX, "gy", "gz"),
        ),
        out_specs=(P(None, GX, "gy", "gz"), P(), P()),
        check_vma=False,
    )
```

```python
import functools

import jax
import jax.numpy as jnp
from jax import lax
from jax.experimental import pallas as pl
from jax.experimental.pallas import tpu as pltpu
from jax.sharding import Mesh, PartitionSpec as P

GX = ("y", "core")
SCATTER = ("core", "gy")
REST = ("y", "gz")
HIGHEST = lax.Precision.HIGHEST
F32 = jnp.float32
BF16 = jnp.bfloat16


def shifted(value, axis, forward):
    size = lax.axis_size(axis)
    up = [(i, (i + 1) % size) for i in range(size - 1)]
    pairs = up if forward else [(j, i) for i, j in up]
    return lax.ppermute(value, axis, pairs)


def trade(up, down, axis):
    return shifted(up, axis, True), shifted(down, axis, False)


def across(ref, a, b):
    fields, span_x, span_y, span_z = ref.shape
    rows = ref.reshape(fields * span_x * span_y, span_z)
    return rows.at[pl.ds(a * span_y + b, fields, stride=span_x * span_y), :]


class Rows:
    def __init__(self, **sizes):
        self.at, self.total = {}, 0
        for name, size in sizes.items():
            self.at[name] = slice(self.total, self.total + size)
            self.total += -(-size // 8) * 8

    def __getitem__(self, name):
        return self.at[name]


def layouts(shape):
    fields, span_x, span_y, _ = shape
    packed = fields * span_x * span_y // 128
    along_z = Rows(near=packed, far=packed, theta=1, theta_far=1, reaction=1)
    along_y = Rows(
        near=span_x * fields, far=span_x * fields, theta=span_x, theta_far=span_x, reaction=span_x,
        z_before=packed, z_after=packed, theta_z_before=1, theta_z_after=1,
    )
    along_x = Rows(
        near=fields * span_y, far=fields * span_y, theta=span_y, theta_far=span_y, reaction=span_y,
        y_before=fields, y_after=fields, theta_y_before=1, theta_y_after=1,
        z_before=packed, z_after=packed, theta_z_before=1, theta_z_after=1,
    )
    return along_x, along_y, along_z


def z_kernel(noise_hbm, theta_hbm, reaction_hbm, noise, theta, reaction, up, down, sem):
    loads = [
        pltpu.make_async_copy(source, target, sem.at[k])
        for k, (source, target) in enumerate(
            ((noise_hbm, noise), (theta_hbm, theta), (reaction_hbm, reaction))
        )
    ]
    for load in loads:
        load.start()
    for load in loads:
        load.wait()
    fields, span_x, span_y, span_z = noise.shape
    rows = layouts(noise.shape)[2]
    step = span_x * span_y
    per = 128 // step
    last = span_z - 1
    for k in range(fields // per):
        turned = noise[k * per : (k + 1) * per].reshape(128, span_z).T
        for name, low in (("near", 0), ("far", 1)):
            at = rows[name].start + k
            down[at : at + 1] = turned[low : low + 1]
            up[at : at + 1] = turned[last - low : last - low + 1]
    for ref, names in ((theta, ("theta", "theta_far")), (reaction, ("reaction",))):
        turned = jnp.concatenate([ref[...].reshape(step, span_z)] * per, axis=0).T
        for low, name in enumerate(names):
            down[rows[name]] = turned[low : low + 1]
            up[rows[name]] = turned[last - low : last - low + 1]


def y_kernel(noise, theta, reaction, z_before, z_after, up, down):
    fields, span_x, span_y, _ = noise.shape
    _, rows, z_rows = layouts(noise.shape)
    for out, near, far in ((up, span_y - 1, span_y - 2), (down, 0, 1)):
        for a in range(span_x):
            at = a * fields
            out[at : at + fields] = across(noise, a, near)[...]
            at = rows["far"].start + a * fields
            out[at : at + fields] = across(noise, a, far)[...]
        out[rows["theta"]] = theta[:, near, :]
        out[rows["theta_far"]] = theta[:, far, :]
        out[rows["reaction"]] = reaction[:, near, :]
        out[rows["z_before"]] = z_before[z_rows["near"]]
        out[rows["z_after"]] = z_after[z_rows["near"]]
        out[rows["theta_z_before"]] = z_before[z_rows["theta"]]
        out[rows["theta_z_after"]] = z_after[z_rows["theta"]]


def x_kernel(noise, theta, reaction, y_before, y_after, z_before, z_after, up, down):
    fields, span_x, span_y, span_z = noise.shape
    rows, y_rows, z_rows = layouts(noise.shape)
    for out, near, far in ((up, span_x - 1, span_x - 2), (down, 0, 1)):
        out[rows["near"]] = noise[:, near].reshape(fields * span_y, span_z)
        out[rows["far"]] = noise[:, far].reshape(fields * span_y, span_z)
        out[rows["theta"]] = theta[near]
        out[rows["theta_far"]] = theta[far]
        out[rows["reaction"]] = reaction[near]
        for name, ref in (("y_before", y_before), ("y_after", y_after)):
            out[rows[name]] = ref[near * fields : (near + 1) * fields]
            at = y_rows["theta"].start + near
            out[rows["theta_" + name]] = ref[at : at + 1]
        for name, ref in (("z_before", z_before), ("z_after", z_after)):
            out[rows[name]] = ref[z_rows["near"]]
            out[rows["theta_" + name]] = ref[z_rows["theta"]]


def turned_out(low, high):
    first = lax.broadcasted_iota(jnp.int32, (128, 128), 0) < 64
    return jnp.where(first, jnp.broadcast_to(low, (128, 128)), jnp.broadcast_to(high, (128, 128))).T


def lane_pair(value, edge):
    last = value.shape[-1] - 1
    axis = value.ndim - 1
    lane = lax.broadcasted_iota(jnp.int32, value.shape, axis)
    return (
        jnp.where(lane == last, edge, pltpu.roll(value, last, axis)),
        jnp.where(lane == 0, edge, pltpu.roll(value, 1, axis)),
    )


def row_pair(value, before, after):
    last = value.shape[-2] - 1
    axis = value.ndim - 2
    row = lax.broadcasted_iota(jnp.int32, value.shape, axis)
    return (
        jnp.where(row == last, after, pltpu.roll(value, last, axis)),
        jnp.where(row == 0, before, pltpu.roll(value, 1, axis)),
    )


def slab_pair(value, before, after, axis):
    size = value.shape[axis]
    return (
        jnp.concatenate([lax.slice_in_dim(value, 1, size, axis=axis), after], axis=axis),
        jnp.concatenate([before, lax.slice_in_dim(value, 0, size - 1, axis=axis)], axis=axis),
    )


def faces_of(theta, others):
    return [0.5 * (theta + other) for other in others]


def diagonal_of(reaction, faces):
    for face in faces:
        reaction = reaction + face
    return reaction


def apply_operator(value, reaction, faces, others):
    result = reaction * value
    for face, other in zip(faces, others):
        result = result + face * (value - other)
    return result


def inside(theta, diagonal):
    on = theta > 0.0
    return jnp.where(on, 1.0 / jnp.where(on, diagonal, 1.0), 0.0)


def operator_kernel(
    noise, theta, reaction, xb, xa, yb, ya, zb, za, z_up, z_down, own, scaled, image, y_out, y_in, y_before_z, y_after_z
):
    fields, span_x, span_y, span_z = noise.shape
    xr, yr, zr = layouts(noise.shape)
    step = span_x * span_y
    per = 128 // step
    blocks = fields // per
    block = (per, span_x, span_y, span_z)
    slab = (fields, 1, span_y, span_z)

    def z_edges(before, after, k):
        return turned_out(before[k : k + 1], after[k : k + 1]).reshape(block)

    for a in range(span_x):
        at = slice(a * fields, (a + 1) * fields)
        across(y_out, 1 + a, 0)[...] = yb[at]
        across(y_out, 1 + a, span_y - 1)[...] = ya[at]
    for a, ref in ((0, xb), (span_x + 1, xa)):
        across(y_out, a, 0)[...] = ref[xr["y_before"]]
        across(y_out, a, span_y - 1)[...] = ref[xr["y_after"]]

    def z_theta(ref, rows):
        return turned_out(ref[rows["theta_z_before"]], ref[rows["theta_z_after"]]).reshape(block)[0]

    wide = jnp.concatenate([xb[xr["theta"]][None], theta[...], xa[xr["theta"]][None]], axis=0)
    wide_reaction = jnp.concatenate([xb[xr["reaction"]][None], reaction[...], xa[xr["reaction"]][None]], axis=0)
    edge = turned_out(zb[zr["theta"]], za[zr["theta"]]).reshape(block)[0]
    edge = jnp.concatenate([z_theta(xb, xr)[span_x - 1 :], edge, z_theta(xa, xr)[:1]], axis=0)
    rows_before = jnp.concatenate([xb[xr["theta_y_before"]], yb[yr["theta"]], xa[xr["theta_y_before"]]], axis=0)
    rows_after = jnp.concatenate([xb[xr["theta_y_after"]], ya[yr["theta"]], xa[xr["theta_y_after"]]], axis=0)
    faces = faces_of(
        wide,
        slab_pair(wide, xb[xr["theta_far"]][None], xa[xr["theta_far"]][None], 0)
        + row_pair(wide, rows_before[:, None], rows_after[:, None])
        + lane_pair(wide, edge),
    )
    inverse = inside(wide, diagonal_of(wide_reaction, faces))

    for k in range(blocks):
        at = slice(k * per, (k + 1) * per)
        slab_rows = slice(k * per * span_y, (k + 1) * per * span_y)
        far_rows = slice(xr["far"].start + slab_rows.start, xr["far"].start + slab_rows.stop)
        part = (per, 1, span_y, span_z)
        value = jnp.concatenate(
            [xb[slab_rows].reshape(part), noise[at], xa[slab_rows].reshape(part)], axis=1
        )
        edge = jnp.concatenate(
            [
                z_edges(xb[xr["z_before"]], xb[xr["z_after"]], k)[:, span_x - 1 :],
                z_edges(zb[zr["near"]], za[zr["near"]], k),
                z_edges(xa[xr["z_before"]], xa[xr["z_after"]], k)[:, :1],
            ],
            axis=1,
        )
        others = (
            slab_pair(value, xb[far_rows].reshape(part), xa[far_rows].reshape(part), 1)
            + row_pair(value, y_out[at], y_out[at])
            + lane_pair(value, edge)
        )
        scaled[at] = apply_operator(value, wide_reaction, faces, others) * inverse
        y_before_z[at] = z_edges(yb[yr["z_before"]], yb[yr["z_after"]], k)
        y_after_z[at] = z_edges(ya[yr["z_before"]], ya[yr["z_after"]], k)

    def along_y(ref, edges, at_edge, at_own, name, before):
        shape = (span_x, fields, span_z)
        value = ref[yr["near"]].reshape(shape)
        far = ref[yr["far"]].reshape(shape)
        inner = jnp.stack([across(noise, a, at_own)[...] for a in range(span_x)])
        edge = jnp.stack([across(edges, a, at_edge)[...] for a in range(span_x)])
        others = (
            slab_pair(value, xb[xr[name]][None], xa[xr[name]][None], 0)
            + ((inner, far) if before else (far, inner))
            + lane_pair(value, edge)
        )
        here = ref[yr["theta"]][:, None]
        inner = theta[:, at_own, :][:, None]
        far = ref[yr["theta_far"]][:, None]
        edge = z_theta(ref, yr)[:, at_edge, :][:, None]
        sides = ref[yr["reaction"]][:, None]
        name = "theta_" + name
        values = faces_of(
            here,
            slab_pair(here, xb[xr[name]][None], xa[xr[name]][None], 0)
            + ((inner, far) if before else (far, inner))
            + lane_pair(here, edge),
        )
        result = apply_operator(value, sides, values, others) * inside(here, diagonal_of(sides, values))
        for a in range(span_x):
            across(y_in, a, at_own)[...] = result[a]

    along_y(yb, y_before_z, span_y - 1, 0, "y_before", True)
    along_y(ya, y_after_z, 0, span_y - 1, "y_after", False)

    def along_z(ref, own_ref, name, before):
        def others_of(value, x_before, x_after, y_before, y_after, far, inner):
            lane = lax.broadcasted_iota(jnp.int32, value.shape, 1)
            at_y = lane % span_y
            at_x = (lane // span_y) % span_x
            corner = step - span_y
            return (
                jnp.where(at_x == span_x - 1, pltpu.roll(x_after, corner, 1), pltpu.roll(value, 128 - span_y, 1)),
                jnp.where(at_x == 0, pltpu.roll(x_before, 128 - corner, 1), pltpu.roll(value, span_y, 1)),
                jnp.where(at_y == span_y - 1, pltpu.roll(y_after, span_y - 1, 1), pltpu.roll(value, 127, 1)),
                jnp.where(at_y == 0, pltpu.roll(y_before, 129 - span_y, 1), pltpu.roll(value, 1, 1)),
            ) + ((inner, far) if before else (far, inner))

        value = ref[zr["near"]]
        others = others_of(
            value, xb[xr[name]], xa[xr[name]], yb[yr[name]], ya[yr[name]], ref[zr["far"]], own_ref[zr["near"]]
        )
        name = "theta_" + name
        many = (8, 128)

        def row(source, at):
            return jnp.broadcast_to(source[at], many)

        here = row(ref, zr["theta"])
        sides = row(ref, zr["reaction"])
        values = faces_of(
            here,
            others_of(
                here, row(xb, xr[name]), row(xa, xr[name]), row(yb, yr[name]), row(ya, yr[name]),
                row(ref, zr["theta_far"]), row(own_ref, zr["theta"]),
            ),
        )
        values = [face[:1] for face in values]
        here, sides = here[:1], sides[:1]
        return apply_operator(value, sides, values, others) * inside(here, diagonal_of(sides, values))

    z_low = along_z(zb, z_down, "z_before", True)
    z_high = along_z(za, z_up, "z_after", False)

    faces = [face[1 : 1 + span_x] for face in faces]
    for k in range(blocks):
        at = slice(k * per, (k + 1) * per)
        value = scaled[at, 1 : 1 + span_x]
        others = (
            (scaled[at, 2 : 2 + span_x], scaled[at, :span_x])
            + row_pair(value, y_in[at], y_in[at])
            + lane_pair(value, z_edges(z_low, z_high, k))
        )
        image[at] = apply_operator(value, reaction[...], faces, others)
    for a in range(span_x):
        for b in range(span_y):
            at = (a * span_y + b) * span_z
            own[:fields, at : at + span_z], own[fields:, at : at + span_z] = split(across(image, a, b)[...])


def split(value):
    high = value.astype(BF16)
    return high, (value - high.astype(F32)).astype(BF16)


def stacked(value):
    return jnp.concatenate(split(value), axis=0)


def contract(left, right, dims):
    return lax.dot_general(left, right, ((dims[0], dims[1]), ((), ())), preferred_element_type=F32)


def exact(left, right, dims):
    return lax.dot_general(
        left, right, ((dims[0], dims[1]), ((), ())), precision=HIGHEST, preferred_element_type=F32
    )


ROWS = ((1,), (1,))
PLAIN = ((1,), (0,))
COLUMNS = ((0,), (0,))


def basis_kernel(basis_hbm, high, low, packed, basis, sem):
    stored, span_x, span_y, span_z = basis.shape
    chunk = stored // sem.shape[0]
    loads = [
        pltpu.make_async_copy(basis_hbm.at[pl.ds(k * chunk, chunk)], basis.at[pl.ds(k * chunk, chunk)], sem.at[k])
        for k in range(sem.shape[0])
    ]
    for load in loads:
        load.start()
    for k, load in enumerate(loads):
        load.wait()
        part = basis.at[pl.ds(k * chunk, chunk)]
        rows = slice(k * chunk, (k + 1) * chunk)
        for a in range(span_x):
            for b in range(span_y):
                at = (a * span_y + b) * span_z
                high[rows, at : at + span_z], low[rows, at : at + span_z] = split(across(part, a, b)[...])
    top, rest = high[...], low[...]
    cross = contract(top, rest, ROWS)
    gram = contract(top, top, ROWS) + contract(rest, rest, ROWS) + (cross + cross.T)
    third = stored // 3
    packed[:third] = jnp.concatenate([gram[:third, :third], gram[2 * third :, 2 * third :]], axis=1)
    packed[third:] = gram[third:, : 2 * third]


def product_kernel(gram, high, low, own, packed):
    stored, fields = high.shape[0], own.shape[0] // 2
    both = own[...]
    product = contract(high[...], both, ROWS) + contract(low[...], both, ROWS)
    product = product[:, :fields] + product[:, fields:]
    square = contract(both, both, ROWS)
    square = square[:fields] + square[fields:]
    square = square[:, :fields] + square[:, fields:]
    third = stored // 3
    last = jnp.concatenate([square, jnp.zeros((third - fields, fields), F32)], axis=0)
    packed[:stored] = gram[...]
    packed[stored:] = jnp.concatenate(
        [product[:third], product[third : 2 * third], product[2 * third : stored], last], axis=1
    )


def eliminate(square, right):
    size = square.shape[0]
    work = jnp.concatenate([0.5 * (square + square.T), right], axis=1)
    row = lax.broadcasted_iota(jnp.int32, work.shape, 0)
    lane = lax.broadcasted_iota(jnp.int32, work.shape, 1)
    for start in range(0, size, 8):
        columns = [jnp.broadcast_to(work[:, k : k + 1], work.shape) for k in range(start, start + 8)]
        for at in range(8):
            k = start + at
            inverse = 1.0 / columns[at][k : k + 1]
            below = jnp.where(row > k, columns[at], 0.0)
            work = work - below * (work[k : k + 1] * inverse)
            for later in range(at + 1, 8):
                columns[later] = columns[later] - below * (columns[later][k : k + 1] * inverse)
    scale = jnp.sum(jnp.where(lane == row, work, 0.0), axis=1, keepdims=True)
    work = work / jnp.sqrt(scale)
    upper = jnp.where(lane >= row, work, 0.0)[:, :size]
    return upper, work[:, size:]


def finish_kernel(packed, high, low, image_hbm, new_block, factor, projection, image, sem, *, cells):
    load = pltpu.make_async_copy(image_hbm, image, sem)
    load.start()
    fields, span_x, span_y, span_z = new_block.shape
    stored = high.shape[0]
    third = stored // 3
    scaled = packed[...] * (1.0 / cells)
    top, body, tail = scaled[:third], scaled[third:stored], scaled[stored:]
    middle = body[:third, third:]
    first = jnp.concatenate([top[:, :third], body[:, :third].T], axis=1)
    second = jnp.concatenate([body[:third, :third], middle, body[third:, third:].T], axis=1)
    last = jnp.concatenate([body[third:], top[:, third:]], axis=1)
    gram = jnp.concatenate([first, second, last], axis=0)
    one = jnp.concatenate([tail[:, k * fields : (k + 1) * fields] for k in range(3)], axis=0)
    own = tail[:fields, 3 * fields :]
    two = one - exact(gram, one, PLAIN)
    left_over = two - exact(gram, two, PLAIN)
    both = one + two
    square = own - exact(one, both, COLUMNS) - exact(both, left_over, COLUMNS)
    row = lax.broadcasted_iota(jnp.int32, (fields, fields), 0)
    lane = lax.broadcasted_iota(jnp.int32, (fields, fields), 1)
    upper_one, inverse_one = eliminate(square, jnp.where(row == lane, 1.0, 0.0))
    again = exact(exact(inverse_one, 0.5 * (square + square.T), PLAIN), inverse_one, ROWS)
    upper_two, inverse = eliminate(again, inverse_one)
    factor[...] = exact(upper_two, upper_one, PLAIN)
    projection[...] = both.T
    mixed = stacked(exact(inverse, both, ROWS))
    inverse = stacked(inverse)
    width = span_y * span_z
    load.wait()
    for a in range(span_x):
        at = a * width
        part = contract(inverse, image[:fields, at : at + width], PLAIN)
        part = part + contract(inverse, image[fields:, at : at + width], PLAIN)
        part = part - contract(mixed, high[:, at : at + width], PLAIN)
        part = part - contract(mixed, low[:, at : at + width], PLAIN)
        value = part[:fields] + part[fields:]
        for b in range(span_y):
            across(new_block, a, b)[...] = value[:, b * span_z : (b + 1) * span_z]


def call(kernel, outs, *args, scratch=(), hbm=(), limit=16, cost=1 << 21):
    return pl.pallas_call(
        kernel,
        out_shape=[o if isinstance(o, jax.ShapeDtypeStruct) else jax.ShapeDtypeStruct(o, F32) for o in outs],
        in_specs=[pl.BlockSpec(memory_space=pltpu.HBM if k in hbm else pltpu.VMEM) for k in range(len(args))],
        out_specs=[pl.BlockSpec(memory_space=pltpu.VMEM)] * len(outs),
        scratch_shapes=list(scratch),
        compiler_params=pltpu.CompilerParams(vmem_limit_bytes=limit << 20),
        cost_estimate=pl.CostEstimate(flops=1 << 22, bytes_accessed=cost, transcendentals=0),
    )(*(pltpu.with_memory_space_constraint(a, pltpu.HBM) if k in hbm else a for k, a in enumerate(args)))


def spread_sum(value, axes):
    size = lax.axis_size(axes)
    copies = jnp.broadcast_to(value[None], (size,) + value.shape)
    return jnp.sum(lax.all_to_all(copies, axes, 0, 0), axis=0)


def total(rows):
    size = lax.axis_size(SCATTER)
    pieces = rows.reshape(size, -1, rows.shape[1])
    piece = jnp.sum(lax.all_to_all(pieces, SCATTER, 0, 0), axis=0)
    piece = spread_sum(piece, REST)
    copies = jnp.broadcast_to(piece[None], (size,) + piece.shape)
    return lax.all_to_all(copies, SCATTER, 0, 0).reshape(rows.shape)


def shards(noise, basis, conductivity, reaction):
    columns = noise.shape[0]
    shape = noise.shape
    stored = basis.shape[0]
    cell_total = float(
        shape[1] * shape[2] * shape[3] * lax.axis_size(GX) * lax.axis_size("gy") * lax.axis_size("gz")
    )
    x_rows, y_rows, z_rows = [[(rows.total, 128)] * 2 for rows in layouts(shape)]
    noise, conductivity, reaction, z_up, z_down = call(
        z_kernel,
        [shape, conductivity.shape, reaction.shape] + z_rows,
        noise,
        conductivity,
        reaction,
        scratch=(pltpu.SemaphoreType.DMA((3,)),),
        hbm=(0, 1, 2),
    )
    fields = (noise, conductivity, reaction)
    z_halo = trade(z_up, z_down, "gz")
    y_halo = trade(*call(y_kernel, y_rows, *fields, *z_halo), "gy")
    x_halo = trade(*call(x_kernel, x_rows, *fields, *y_halo, *z_halo), GX)
    cells = shape[1] * shape[2] * shape[3]
    third = stored // 3
    wide = jax.ShapeDtypeStruct((stored, cells), BF16)
    high, low, gram = call(
        basis_kernel,
        [wide, wide, (stored, 2 * third)],
        basis,
        scratch=(pltpu.VMEM(basis.shape, F32), pltpu.SemaphoreType.DMA((6,))),
        hbm=(0,),
    )
    (own,) = call(
        operator_kernel,
        [jax.ShapeDtypeStruct((2 * columns, cells), BF16)],
        *fields,
        *x_halo,
        *y_halo,
        *z_halo,
        z_up,
        z_down,
        scratch=[
            pltpu.VMEM((columns, span, *shape[2:]), F32)
            for span in (shape[1] + 2, shape[1], shape[1] + 2, shape[1], shape[1], shape[1])
        ],
    )
    (packed,) = call(product_kernel, [(stored + third, 2 * third)], gram, high, low, own)
    new_block, factor, projection = call(
        functools.partial(finish_kernel, cells=cell_total),
        [shape, (columns, columns), (columns, stored)],
        total(packed),
        high,
        low,
        own,
        scratch=(pltpu.VMEM(own.shape, BF16), pltpu.SemaphoreType.DMA),
        hbm=(3,),
    )
    return (new_block, factor, projection.T)


def solution(mesh):
    grid = mesh.devices.reshape(mesh.devices.shape[0] // 2, 2, *mesh.devices.shape[1:])
    fine = Mesh(grid, ("y", "core", "gy", "gz"))
    return jax.shard_map(
        shards,
        mesh=fine,
        in_specs=(
            P(None, GX, "gy", "gz"),
            P(None, GX, "gy", "gz"),
            P(GX, "gy", "gz"),
            P(GX, "gy", "gz"),
        ),
        out_specs=(P(None, GX, "gy", "gz"), P(), P()),
        check_vma=False,
    )
```

```python
import functools

import jax
import jax.numpy as jnp
from jax import lax
from jax.experimental import pallas as pl
from jax.experimental.pallas import tpu as pltpu
from jax.sharding import Mesh, PartitionSpec as P

GX = ("y", "core")
SCATTER = ("core", "gy")
REST = ("y", "gz")
HIGHEST = lax.Precision.HIGHEST
F32 = jnp.float32
BF16 = jnp.bfloat16


def trade(inner, outer, axis):
    size = lax.axis_size(axis)
    swaps = [[(i, i + 1) for i in range(start, size - 1, 2)] for start in (0, 1)]
    swaps = [pairs + [(j, i) for i, j in pairs] for pairs in swaps]
    inner = lax.ppermute(inner, axis, swaps[0])
    return inner, lax.ppermute(outer, axis, swaps[1])


def first_of_pair(axis):
    return lax.axis_index(axis) % 2 == 0


def faces_to(axis, inner, outer, store):
    @pl.when(first_of_pair(axis))
    def _():
        store(inner, outer)

    @pl.when(jnp.logical_not(first_of_pair(axis)))
    def _():
        store(outer, inner)


def sides(axis, inner, outer):
    first = first_of_pair(axis)
    return jnp.where(first, outer[...], inner[...]), jnp.where(first, inner[...], outer[...])


def across(ref, a, b):
    fields, span_x, span_y, span_z = ref.shape
    rows = ref.reshape(fields * span_x * span_y, span_z)
    return rows.at[pl.ds(a * span_y + b, fields, stride=span_x * span_y), :]


class Rows:
    def __init__(self, **sizes):
        self.at, self.total = {}, 0
        for name, size in sizes.items():
            self.at[name] = slice(self.total, self.total + size)
            self.total += -(-size // 8) * 8

    def __getitem__(self, name):
        return self.at[name]


def layouts(shape):
    fields, span_x, span_y, _ = shape
    packed = fields * span_x * span_y // 128
    along_z = Rows(near=packed, far=packed, theta=1, theta_far=1, reaction=1)
    along_y = Rows(
        near=span_x * fields, far=span_x * fields, theta=span_x, theta_far=span_x, reaction=span_x,
        z_before=packed, z_after=packed, theta_z_before=1, theta_z_after=1,
    )
    along_x = Rows(
        near=fields * span_y, far=fields * span_y, theta=span_y, theta_far=span_y, reaction=span_y,
        y_before=fields, y_after=fields, theta_y_before=1, theta_y_after=1,
        z_before=packed, z_after=packed, theta_z_before=1, theta_z_after=1,
    )
    return along_x, along_y, along_z


def z_kernel(noise_hbm, theta_hbm, reaction_hbm, noise, theta, reaction, up, down, inner, outer, sem):
    loads = [
        pltpu.make_async_copy(source, target, sem.at[k])
        for k, (source, target) in enumerate(
            ((noise_hbm, noise), (theta_hbm, theta), (reaction_hbm, reaction))
        )
    ]
    for load in loads:
        load.start()
    for load in loads:
        load.wait()
    fields, span_x, span_y, span_z = noise.shape
    rows = layouts(noise.shape)[2]
    step = span_x * span_y
    per = 128 // step
    last = span_z - 1
    for k in range(fields // per):
        turned = noise[k * per : (k + 1) * per].reshape(128, span_z).T
        for name, low in (("near", 0), ("far", 1)):
            at = rows[name].start + k
            down[at : at + 1] = turned[low : low + 1]
            up[at : at + 1] = turned[last - low : last - low + 1]
    for ref, names in ((theta, ("theta", "theta_far")), (reaction, ("reaction",))):
        turned = jnp.concatenate([ref[...].reshape(step, span_z)] * per, axis=0).T
        for low, name in enumerate(names):
            down[rows[name]] = turned[low : low + 1]
            up[rows[name]] = turned[last - low : last - low + 1]

    def store(above, below):
        above[...] = up[...]
        below[...] = down[...]

    faces_to("gz", inner, outer, store)


def y_kernel(noise, theta, reaction, z_inner, z_outer, inner, outer):
    z_before, z_after = sides("gz", z_inner, z_outer)
    fields, span_x, span_y, _ = noise.shape
    _, rows, z_rows = layouts(noise.shape)

    def store(up, down):
        for out, near, far in ((up, span_y - 1, span_y - 2), (down, 0, 1)):
            for a in range(span_x):
                at = a * fields
                out[at : at + fields] = across(noise, a, near)[...]
                at = rows["far"].start + a * fields
                out[at : at + fields] = across(noise, a, far)[...]
            out[rows["theta"]] = theta[:, near, :]
            out[rows["theta_far"]] = theta[:, far, :]
            out[rows["reaction"]] = reaction[:, near, :]
            out[rows["z_before"]] = z_before[z_rows["near"]]
            out[rows["z_after"]] = z_after[z_rows["near"]]
            out[rows["theta_z_before"]] = z_before[z_rows["theta"]]
            out[rows["theta_z_after"]] = z_after[z_rows["theta"]]

    faces_to("gy", inner, outer, store)


def x_kernel(noise, theta, reaction, y_inner, y_outer, z_inner, z_outer, inner, outer):
    y_before, y_after = sides("gy", y_inner, y_outer)
    z_before, z_after = sides("gz", z_inner, z_outer)
    fields, span_x, span_y, span_z = noise.shape
    rows, y_rows, z_rows = layouts(noise.shape)

    def store(up, down):
        for out, near, far in ((up, span_x - 1, span_x - 2), (down, 0, 1)):
            out[rows["near"]] = noise[:, near].reshape(fields * span_y, span_z)
            out[rows["far"]] = noise[:, far].reshape(fields * span_y, span_z)
            out[rows["theta"]] = theta[near]
            out[rows["theta_far"]] = theta[far]
            out[rows["reaction"]] = reaction[near]
            for name, ref in (("y_before", y_before), ("y_after", y_after)):
                out[rows[name]] = ref[near * fields : (near + 1) * fields]
                at = y_rows["theta"].start + near
                out[rows["theta_" + name]] = ref[at : at + 1]
            for name, ref in (("z_before", z_before), ("z_after", z_after)):
                out[rows[name]] = ref[z_rows["near"]]
                out[rows["theta_" + name]] = ref[z_rows["theta"]]

    faces_to(GX, inner, outer, store)


def turned_out(low, high):
    first = lax.broadcasted_iota(jnp.int32, (128, 128), 0) < 64
    return jnp.where(first, jnp.broadcast_to(low, (128, 128)), jnp.broadcast_to(high, (128, 128))).T


def lane_pair(value, edge):
    last = value.shape[-1] - 1
    axis = value.ndim - 1
    lane = lax.broadcasted_iota(jnp.int32, value.shape, axis)
    return (
        jnp.where(lane == last, edge, pltpu.roll(value, last, axis)),
        jnp.where(lane == 0, edge, pltpu.roll(value, 1, axis)),
    )


def row_pair(value, before, after):
    last = value.shape[-2] - 1
    axis = value.ndim - 2
    row = lax.broadcasted_iota(jnp.int32, value.shape, axis)
    return (
        jnp.where(row == last, after, pltpu.roll(value, last, axis)),
        jnp.where(row == 0, before, pltpu.roll(value, 1, axis)),
    )


def slab_pair(value, before, after, axis):
    size = value.shape[axis]
    return (
        jnp.concatenate([lax.slice_in_dim(value, 1, size, axis=axis), after], axis=axis),
        jnp.concatenate([before, lax.slice_in_dim(value, 0, size - 1, axis=axis)], axis=axis),
    )


def faces_of(theta, others):
    return [0.5 * (theta + other) for other in others]


def diagonal_of(reaction, faces):
    for face in faces:
        reaction = reaction + face
    return reaction


def apply_operator(value, reaction, faces, others):
    result = reaction * value
    for face, other in zip(faces, others):
        result = result + face * (value - other)
    return result


def inside(theta, diagonal):
    on = theta > 0.0
    return jnp.where(on, 1.0 / jnp.where(on, diagonal, 1.0), 0.0)


def operator_kernel(
    noise, theta, reaction, x_inner, x_outer, y_inner, y_outer, z_inner, z_outer, z_up, z_down, own, scaled, image,
    y_out, y_in, y_before_z, y_after_z, xb, xa, yb, ya, zb, za
):
    xb[...], xa[...] = sides(GX, x_inner, x_outer)
    yb[...], ya[...] = sides("gy", y_inner, y_outer)
    zb[...], za[...] = sides("gz", z_inner, z_outer)
    fields, span_x, span_y, span_z = noise.shape
    xr, yr, zr = layouts(noise.shape)
    step = span_x * span_y
    per = 128 // step
    blocks = fields // per
    block = (per, span_x, span_y, span_z)
    slab = (fields, 1, span_y, span_z)

    def z_edges(before, after, k):
        return turned_out(before[k : k + 1], after[k : k + 1]).reshape(block)

    for a in range(span_x):
        at = slice(a * fields, (a + 1) * fields)
        across(y_out, 1 + a, 0)[...] = yb[at]
        across(y_out, 1 + a, span_y - 1)[...] = ya[at]
    for a, ref in ((0, xb), (span_x + 1, xa)):
        across(y_out, a, 0)[...] = ref[xr["y_before"]]
        across(y_out, a, span_y - 1)[...] = ref[xr["y_after"]]

    def z_theta(ref, rows):
        return turned_out(ref[rows["theta_z_before"]], ref[rows["theta_z_after"]]).reshape(block)[0]

    wide = jnp.concatenate([xb[xr["theta"]][None], theta[...], xa[xr["theta"]][None]], axis=0)
    wide_reaction = jnp.concatenate([xb[xr["reaction"]][None], reaction[...], xa[xr["reaction"]][None]], axis=0)
    edge = turned_out(zb[zr["theta"]], za[zr["theta"]]).reshape(block)[0]
    edge = jnp.concatenate([z_theta(xb, xr)[span_x - 1 :], edge, z_theta(xa, xr)[:1]], axis=0)
    rows_before = jnp.concatenate([xb[xr["theta_y_before"]], yb[yr["theta"]], xa[xr["theta_y_before"]]], axis=0)
    rows_after = jnp.concatenate([xb[xr["theta_y_after"]], ya[yr["theta"]], xa[xr["theta_y_after"]]], axis=0)
    faces = faces_of(
        wide,
        slab_pair(wide, xb[xr["theta_far"]][None], xa[xr["theta_far"]][None], 0)
        + row_pair(wide, rows_before[:, None], rows_after[:, None])
        + lane_pair(wide, edge),
    )
    inverse = inside(wide, diagonal_of(wide_reaction, faces))

    for k in range(blocks):
        at = slice(k * per, (k + 1) * per)
        slab_rows = slice(k * per * span_y, (k + 1) * per * span_y)
        far_rows = slice(xr["far"].start + slab_rows.start, xr["far"].start + slab_rows.stop)
        part = (per, 1, span_y, span_z)
        value = jnp.concatenate(
            [xb[slab_rows].reshape(part), noise[at], xa[slab_rows].reshape(part)], axis=1
        )
        edge = jnp.concatenate(
            [
                z_edges(xb[xr["z_before"]], xb[xr["z_after"]], k)[:, span_x - 1 :],
                z_edges(zb[zr["near"]], za[zr["near"]], k),
                z_edges(xa[xr["z_before"]], xa[xr["z_after"]], k)[:, :1],
            ],
            axis=1,
        )
        others = (
            slab_pair(value, xb[far_rows].reshape(part), xa[far_rows].reshape(part), 1)
            + row_pair(value, y_out[at], y_out[at])
            + lane_pair(value, edge)
        )
        scaled[at] = apply_operator(value, wide_reaction, faces, others) * inverse
        y_before_z[at] = z_edges(yb[yr["z_before"]], yb[yr["z_after"]], k)
        y_after_z[at] = z_edges(ya[yr["z_before"]], ya[yr["z_after"]], k)

    def along_y(ref, edges, at_edge, at_own, name, before):
        shape = (span_x, fields, span_z)
        value = ref[yr["near"]].reshape(shape)
        far = ref[yr["far"]].reshape(shape)
        inner = jnp.stack([across(noise, a, at_own)[...] for a in range(span_x)])
        edge = jnp.stack([across(edges, a, at_edge)[...] for a in range(span_x)])
        others = (
            slab_pair(value, xb[xr[name]][None], xa[xr[name]][None], 0)
            + ((inner, far) if before else (far, inner))
            + lane_pair(value, edge)
        )
        here = ref[yr["theta"]][:, None]
        inner = theta[:, at_own, :][:, None]
        far = ref[yr["theta_far"]][:, None]
        edge = z_theta(ref, yr)[:, at_edge, :][:, None]
        sides = ref[yr["reaction"]][:, None]
        name = "theta_" + name
        values = faces_of(
            here,
            slab_pair(here, xb[xr[name]][None], xa[xr[name]][None], 0)
            + ((inner, far) if before else (far, inner))
            + lane_pair(here, edge),
        )
        result = apply_operator(value, sides, values, others) * inside(here, diagonal_of(sides, values))
        for a in range(span_x):
            across(y_in, a, at_own)[...] = result[a]

    along_y(yb, y_before_z, span_y - 1, 0, "y_before", True)
    along_y(ya, y_after_z, 0, span_y - 1, "y_after", False)

    def along_z(ref, own_ref, name, before):
        def others_of(value, x_before, x_after, y_before, y_after, far, inner):
            lane = lax.broadcasted_iota(jnp.int32, value.shape, 1)
            at_y = lane % span_y
            at_x = (lane // span_y) % span_x
            corner = step - span_y
            return (
                jnp.where(at_x == span_x - 1, pltpu.roll(x_after, corner, 1), pltpu.roll(value, 128 - span_y, 1)),
                jnp.where(at_x == 0, pltpu.roll(x_before, 128 - corner, 1), pltpu.roll(value, span_y, 1)),
                jnp.where(at_y == span_y - 1, pltpu.roll(y_after, span_y - 1, 1), pltpu.roll(value, 127, 1)),
                jnp.where(at_y == 0, pltpu.roll(y_before, 129 - span_y, 1), pltpu.roll(value, 1, 1)),
            ) + ((inner, far) if before else (far, inner))

        value = ref[zr["near"]]
        others = others_of(
            value, xb[xr[name]], xa[xr[name]], yb[yr[name]], ya[yr[name]], ref[zr["far"]], own_ref[zr["near"]]
        )
        name = "theta_" + name
        many = (8, 128)

        def row(source, at):
            return jnp.broadcast_to(source[at], many)

        here = row(ref, zr["theta"])
        sides = row(ref, zr["reaction"])
        values = faces_of(
            here,
            others_of(
                here, row(xb, xr[name]), row(xa, xr[name]), row(yb, yr[name]), row(ya, yr[name]),
                row(ref, zr["theta_far"]), row(own_ref, zr["theta"]),
            ),
        )
        values = [face[:1] for face in values]
        here, sides = here[:1], sides[:1]
        return apply_operator(value, sides, values, others) * inside(here, diagonal_of(sides, values))

    z_low = along_z(zb, z_down, "z_before", True)
    z_high = along_z(za, z_up, "z_after", False)

    faces = [face[1 : 1 + span_x] for face in faces]
    for k in range(blocks):
        at = slice(k * per, (k + 1) * per)
        value = scaled[at, 1 : 1 + span_x]
        others = (
            (scaled[at, 2 : 2 + span_x], scaled[at, :span_x])
            + row_pair(value, y_in[at], y_in[at])
            + lane_pair(value, z_edges(z_low, z_high, k))
        )
        image[at] = apply_operator(value, reaction[...], faces, others)
    for a in range(span_x):
        for b in range(span_y):
            at = (a * span_y + b) * span_z
            own[:fields, at : at + span_z], own[fields:, at : at + span_z] = split(across(image, a, b)[...])


def split(value):
    high = value.astype(BF16)
    return high, (value - high.astype(F32)).astype(BF16)


def stacked(value):
    return jnp.concatenate(split(value), axis=0)


def contract(left, right, dims):
    return lax.dot_general(left, right, ((dims[0], dims[1]), ((), ())), preferred_element_type=F32)


def exact(left, right, dims):
    return lax.dot_general(
        left, right, ((dims[0], dims[1]), ((), ())), precision=HIGHEST, preferred_element_type=F32
    )


ROWS = ((1,), (1,))
PLAIN = ((1,), (0,))
COLUMNS = ((0,), (0,))


def basis_kernel(basis_hbm, high, low, packed, basis, sem):
    stored, span_x, span_y, span_z = basis.shape
    chunk = stored // sem.shape[0]
    loads = [
        pltpu.make_async_copy(basis_hbm.at[pl.ds(k * chunk, chunk)], basis.at[pl.ds(k * chunk, chunk)], sem.at[k])
        for k in range(sem.shape[0])
    ]
    for load in loads:
        load.start()
    for k, load in enumerate(loads):
        load.wait()
        part = basis.at[pl.ds(k * chunk, chunk)]
        rows = slice(k * chunk, (k + 1) * chunk)
        for a in range(span_x):
            for b in range(span_y):
                at = (a * span_y + b) * span_z
                high[rows, at : at + span_z], low[rows, at : at + span_z] = split(across(part, a, b)[...])
    top, rest = high[...], low[...]
    cross = contract(top, rest, ROWS)
    gram = contract(top, top, ROWS) + contract(rest, rest, ROWS) + (cross + cross.T)
    third = stored // 3
    packed[:third] = jnp.concatenate([gram[:third, :third], gram[2 * third :, 2 * third :]], axis=1)
    packed[third:] = gram[third:, : 2 * third]


def product_kernel(gram, high, low, own, packed):
    stored, fields = high.shape[0], own.shape[0] // 2
    both = own[...]
    product = contract(high[...], both, ROWS) + contract(low[...], both, ROWS)
    product = product[:, :fields] + product[:, fields:]
    square = contract(both, both, ROWS)
    square = square[:fields] + square[fields:]
    square = square[:, :fields] + square[:, fields:]
    third = stored // 3
    last = jnp.concatenate([square, jnp.zeros((third - fields, fields), F32)], axis=0)
    packed[:stored] = gram[...]
    packed[stored:] = jnp.concatenate(
        [product[:third], product[third : 2 * third], product[2 * third : stored], last], axis=1
    )


def eliminate(square, right):
    size = square.shape[0]
    work = jnp.concatenate([0.5 * (square + square.T), right], axis=1)
    row = lax.broadcasted_iota(jnp.int32, work.shape, 0)
    lane = lax.broadcasted_iota(jnp.int32, work.shape, 1)
    for start in range(0, size, 8):
        columns = [jnp.broadcast_to(work[:, k : k + 1], work.shape) for k in range(start, start + 8)]
        for at in range(8):
            k = start + at
            inverse = 1.0 / columns[at][k : k + 1]
            below = jnp.where(row > k, columns[at], 0.0)
            work = work - below * (work[k : k + 1] * inverse)
            for later in range(at + 1, 8):
                columns[later] = columns[later] - below * (columns[later][k : k + 1] * inverse)
    scale = jnp.sum(jnp.where(lane == row, work, 0.0), axis=1, keepdims=True)
    work = work / jnp.sqrt(scale)
    upper = jnp.where(lane >= row, work, 0.0)[:, :size]
    return upper, work[:, size:]


def finish_kernel(packed, high, low, image_hbm, new_block, factor, projection, image, sem, *, cells):
    load = pltpu.make_async_copy(image_hbm, image, sem)
    load.start()
    fields, span_x, span_y, span_z = new_block.shape
    stored = high.shape[0]
    third = stored // 3
    scaled = packed[...] * (1.0 / cells)
    top, body, tail = scaled[:third], scaled[third:stored], scaled[stored:]
    middle = body[:third, third:]
    first = jnp.concatenate([top[:, :third], body[:, :third].T], axis=1)
    second = jnp.concatenate([body[:third, :third], middle, body[third:, third:].T], axis=1)
    last = jnp.concatenate([body[third:], top[:, third:]], axis=1)
    gram = jnp.concatenate([first, second, last], axis=0)
    one = jnp.concatenate([tail[:, k * fields : (k + 1) * fields] for k in range(3)], axis=0)
    own = tail[:fields, 3 * fields :]
    two = one - exact(gram, one, PLAIN)
    left_over = two - exact(gram, two, PLAIN)
    both = one + two
    square = own - exact(one, both, COLUMNS) - exact(both, left_over, COLUMNS)
    row = lax.broadcasted_iota(jnp.int32, (fields, fields), 0)
    lane = lax.broadcasted_iota(jnp.int32, (fields, fields), 1)
    upper_one, inverse_one = eliminate(square, jnp.where(row == lane, 1.0, 0.0))
    again = exact(exact(inverse_one, 0.5 * (square + square.T), PLAIN), inverse_one, ROWS)
    upper_two, inverse = eliminate(again, inverse_one)
    factor[...] = exact(upper_two, upper_one, PLAIN)
    projection[...] = both.T
    mixed = stacked(exact(inverse, both, ROWS))
    inverse = stacked(inverse)
    width = span_y * span_z
    load.wait()
    for a in range(span_x):
        at = a * width
        part = contract(inverse, image[:fields, at : at + width], PLAIN)
        part = part + contract(inverse, image[fields:, at : at + width], PLAIN)
        part = part - contract(mixed, high[:, at : at + width], PLAIN)
        part = part - contract(mixed, low[:, at : at + width], PLAIN)
        value = part[:fields] + part[fields:]
        for b in range(span_y):
            across(new_block, a, b)[...] = value[:, b * span_z : (b + 1) * span_z]


def call(kernel, outs, *args, scratch=(), hbm=(), limit=16, cost=1 << 21):
    return pl.pallas_call(
        kernel,
        out_shape=[o if isinstance(o, jax.ShapeDtypeStruct) else jax.ShapeDtypeStruct(o, F32) for o in outs],
        in_specs=[pl.BlockSpec(memory_space=pltpu.HBM if k in hbm else pltpu.VMEM) for k in range(len(args))],
        out_specs=[pl.BlockSpec(memory_space=pltpu.VMEM)] * len(outs),
        scratch_shapes=list(scratch),
        compiler_params=pltpu.CompilerParams(vmem_limit_bytes=limit << 20),
        cost_estimate=pl.CostEstimate(flops=1 << 22, bytes_accessed=cost, transcendentals=0),
    )(*(pltpu.with_memory_space_constraint(a, pltpu.HBM) if k in hbm else a for k, a in enumerate(args)))


def spread_sum(value, axes):
    size = lax.axis_size(axes)
    copies = jnp.broadcast_to(value[None], (size,) + value.shape)
    return jnp.sum(lax.all_to_all(copies, axes, 0, 0), axis=0)


def total(rows):
    size = lax.axis_size(SCATTER)
    pieces = rows.reshape(size, -1, rows.shape[1])
    piece = jnp.sum(lax.all_to_all(pieces, SCATTER, 0, 0), axis=0)
    piece = spread_sum(piece, REST)
    copies = jnp.broadcast_to(piece[None], (size,) + piece.shape)
    return lax.all_to_all(copies, SCATTER, 0, 0).reshape(rows.shape)


def shards(noise, basis, conductivity, reaction):
    columns = noise.shape[0]
    shape = noise.shape
    stored = basis.shape[0]
    cell_total = float(
        shape[1] * shape[2] * shape[3] * lax.axis_size(GX) * lax.axis_size("gy") * lax.axis_size("gz")
    )
    x_rows, y_rows, z_rows = [[(rows.total, 128)] * 2 for rows in layouts(shape)]
    noise, conductivity, reaction, z_up, z_down, *z_faces = call(
        z_kernel,
        [shape, conductivity.shape, reaction.shape] + z_rows + z_rows,
        noise,
        conductivity,
        reaction,
        scratch=(pltpu.SemaphoreType.DMA((3,)),),
        hbm=(0, 1, 2),
    )
    fields = (noise, conductivity, reaction)
    z_halo = trade(*z_faces, "gz")
    y_halo = trade(*call(y_kernel, y_rows, *fields, *z_halo), "gy")
    x_halo = trade(*call(x_kernel, x_rows, *fields, *y_halo, *z_halo), GX)
    cells = shape[1] * shape[2] * shape[3]
    third = stored // 3
    wide = jax.ShapeDtypeStruct((stored, cells), BF16)
    high, low, gram = call(
        basis_kernel,
        [wide, wide, (stored, 2 * third)],
        basis,
        scratch=(pltpu.VMEM(basis.shape, F32), pltpu.SemaphoreType.DMA((6,))),
        hbm=(0,),
    )
    (own,) = call(
        operator_kernel,
        [jax.ShapeDtypeStruct((2 * columns, cells), BF16)],
        *fields,
        *x_halo,
        *y_halo,
        *z_halo,
        z_up,
        z_down,
        scratch=[
            pltpu.VMEM((columns, span, *shape[2:]), F32)
            for span in (shape[1] + 2, shape[1], shape[1] + 2, shape[1], shape[1], shape[1])
        ]
        + [pltpu.VMEM(rows, F32) for rows in x_rows + y_rows + z_rows],
    )
    (packed,) = call(product_kernel, [(stored + third, 2 * third)], gram, high, low, own)
    new_block, factor, projection = call(
        functools.partial(finish_kernel, cells=cell_total),
        [shape, (columns, columns), (columns, stored)],
        total(packed),
        high,
        low,
        own,
        scratch=(pltpu.VMEM(own.shape, BF16), pltpu.SemaphoreType.DMA),
        hbm=(3,),
    )
    return (new_block, factor, projection.T)


def solution(mesh):
    grid = mesh.devices.reshape(mesh.devices.shape[0] // 2, 2, *mesh.devices.shape[1:])
    fine = Mesh(grid, ("y", "core", "gy", "gz"))
    return jax.shard_map(
        shards,
        mesh=fine,
        in_specs=(
            P(None, GX, "gy", "gz"),
            P(None, GX, "gy", "gz"),
            P(GX, "gy", "gz"),
            P(GX, "gy", "gz"),
        ),
        out_specs=(P(None, GX, "gy", "gz"), P(), P()),
        check_vma=False,
    )
```
